32 devices in a mesh: seg: 4 (over y, core), seq: 8 (over z, x).
Axes of the slice: x: 2, y: 2, z: 4, core: 2. Of those that a mesh axis runs over, the one named last changes fastest.
Arguments:
- tokens: bfloat16 [4096, 2048], P(('seg', 'seq')), may hold values from -6 to 6
- tm_mats: bfloat16 [5, 2048, 2048], P(None, ('seg', 'seq')), may hold values from -0.125 to 0.125
- low_rank: bfloat16 [2, 2048, 224], P(None, ('seg', 'seq')), may hold values from -0.6 to 0.6
- channel_parameters: float32 [16, 2048], replicated, may hold values from -12 to 2
- piece_opening_memory: float32 [4, 32, 64, 64], P('seg'), may hold values from -16 to 16
- cm_key: bfloat16 [2048, 7168], P(None, 'seq'), may hold values from -0.125 to 0.125
- cm_value: bfloat16 [7168, 2048], P('seq'), may hold values from -0.0625 to 0.0625
- cm_recept: bfloat16 [2048, 2048], P(None, 'seq'), may hold values from -0.125 to 0.125
- out_grad: bfloat16 [4096, 2048], P(('seg', 'seq')), may hold values from -6 to 6
Outputs:
- block_out: bfloat16 [4096, 2048], P(('seg', 'seq'))
- input_grad: float32 [4096, 2048], P(('seg', 'seq'))
- tm_mats_grad: float32 [5, 2048, 2048], P(None, ('seg', 'seq'))
- low_rank_grad: float32 [2, 2048, 224], P(None, ('seg', 'seq'))
- vectors_grad: float32 [16, 2048], P(None, ('seg', 'seq'))
- cm_key_grad: float32 [2048, 7168], P(None, 'seq')
- cm_value_grad: float32 [7168, 2048], P('seq')
- cm_recept_grad: float32 [2048, 2048], P(None, 'seq')
The draws below stay inside these ranges and needn't reach their ends.
All inputs are finite; a program needn't handle non-finite values.
Results may differ from the reference program's by a relative error of at most 0.025.
Values may be sent and summed in bfloat16 or wider, within the bound.
No kernel may reach another device: no remote copies, remote signals or barrier semaphores. Data moves between devices by JAX's collectives and lax.ppermute only.
A program may use at most 448 MiB of HBM per device.

```python
import math
import jax
import jax.numpy as jnp
from jax import lax

EMBED_BREADTH = 2048
FF = 7168
CHANNEL_GROUP = 64
MIX_RANK = 32
BLOCK = 16
H = 32
LR = 224
SEG_LEN = 1024
SEGS = 4
TOKENS = 4096


def draw_channel_parameters(key, part):
    lookup_series = jax.random.split(key, 7)
    group_count_total = EMBED_BREADTH // CHANNEL_GROUP
    scaling_multiplier_lines = jax.random.uniform(lookup_series[0], (3, EMBED_BREADTH), minval=0.5, maxval=1.5)
    line_offset_entries = jax.random.uniform(lookup_series[1], (3, EMBED_BREADTH), minval=-0.5, maxval=0.5)
    temporal_blend_lines = jax.random.uniform(lookup_series[2], (8, EMBED_BREADTH), minval=0.05, maxval=0.95)
    reward_entries = jax.random.uniform(lookup_series[3], (EMBED_BREADTH,), minval=-1.0, maxval=1.0)
    fast_share = 0.5
    is_fast = jax.random.uniform(lookup_series[4], (group_count_total, 1)) < fast_share
    slow_rate = jax.random.uniform(lookup_series[5], (group_count_total, CHANNEL_GROUP), minval=0.3, maxval=1.5) / SEG_LEN
    fast_rate = jax.random.uniform(lookup_series[6], (group_count_total, CHANNEL_GROUP), minval=0.04, maxval=0.12)
    fading_floor_speed = jnp.log(jnp.where(is_fast, fast_rate, slow_rate)).reshape(EMBED_BREADTH)
    piled_line_entries = [scaling_multiplier_lines[0], line_offset_entries[0], temporal_blend_lines[0], temporal_blend_lines[1], temporal_blend_lines[2], temporal_blend_lines[3], temporal_blend_lines[4], temporal_blend_lines[5], fading_floor_speed, reward_entries, scaling_multiplier_lines[1], line_offset_entries[1], scaling_multiplier_lines[2], line_offset_entries[2], temporal_blend_lines[6], temporal_blend_lines[7]]
    return jnp.stack(piled_line_entries).astype(jnp.float32)


def draw_low_rank(key, part):
    first_key, second_key = jax.random.split(key, 2)
    up_scale = jnp.where(jnp.arange(LR) < 5 * MIX_RANK, 0.08, 0.12)
    down_raw = jax.random.truncated_normal(first_key, -4.0, 4.0, (EMBED_BREADTH, LR))
    up_raw = jax.random.truncated_normal(second_key, -4.0, 4.0, (EMBED_BREADTH, LR))
    down_scale = 1.0 / math.sqrt(EMBED_BREADTH)
    return jnp.stack([down_raw * down_scale, up_raw * up_scale]).astype(jnp.bfloat16)


def block_levels(key, shape, shards, least, high):
    level = 1.0
    for axis_at, parts in shards:
        draws = jax.random.uniform(jax.random.fold_in(jax.random.fold_in(key, 6), axis_at), (parts,), jnp.float32, least / len(shards), high / len(shards))
        level = level * jnp.repeat(jnp.exp(draws), shape[axis_at] // parts).reshape((-1,) + (1,) * (len(shape) - 1 - axis_at))
    return level


def centred(own_key, shape, scale, bound, cuts=(), kind=jnp.bfloat16):
    values = scale * jax.random.normal(own_key, shape, jnp.float32)
    if cuts:
        values = values * block_levels(own_key, shape, cuts, -0.22, 0.18)
    return jnp.clip(values, -bound, bound).astype(kind)


def setup_inputs(seed: int = 0) -> dict:
    streams_of = jax.random.split(jax.random.key(seed), 10)
    tokens = centred(streams_of[0], (TOKENS, EMBED_BREADTH), 1.0, 6.0, ((0, 32),))
    tm_mats = centred(streams_of[1], (5, EMBED_BREADTH, EMBED_BREADTH), EMBED_BREADTH ** -0.5, 0.125, ((1, 32),))
    low_rank = draw_low_rank(jax.random.fold_in(streams_of[9], 71), 0)
    channel_parameters = draw_channel_parameters(jax.random.fold_in(streams_of[9], 71), 0)
    piece_opening_memory = centred(streams_of[4], (SEGS, H, CHANNEL_GROUP, CHANNEL_GROUP), 4.0, 16.0, ((0, 4),), jnp.float32)
    cm_key = centred(streams_of[5], (EMBED_BREADTH, FF), EMBED_BREADTH ** -0.5, 0.125, ((1, 8),))
    cm_value = centred(streams_of[6], (FF, EMBED_BREADTH), FF ** -0.5, 0.0625, ((0, 8),))
    cm_recept = centred(streams_of[7], (EMBED_BREADTH, EMBED_BREADTH), EMBED_BREADTH ** -0.5, 0.125, ((1, 8),))
    out_grad = centred(streams_of[8], (TOKENS, EMBED_BREADTH), 1.0, 6.0, ((0, 32),))
    return {"tokens": tokens, "tm_mats": tm_mats, "low_rank": low_rank, "channel_parameters": channel_parameters, "piece_opening_memory": piece_opening_memory, "cm_key": cm_key, "cm_value": cm_value, "cm_recept": cm_recept, "out_grad": out_grad}


eps_norm = 1e-05
eps_group = 0.00064
exact_matmul_mode = lax.Precision.HIGHEST

@jax.custom_vjp
def low(v):
    return lax.optimization_barrier(v.astype(jnp.bfloat16)).astype(jnp.float32)

@jax.custom_vjp
def low_back(v):
    return v

def low_keep(v):
    return (low(v), None)

def low_pass(kept, grad):
    return (grad,)

def back_keep(v):
    return (v, None)

def back_low(kept, grad):
    return (low(grad),)
low.defvjp(low_keep, low_pass)
low_back.defvjp(back_keep, back_low)

def both_ways(values):
    return low(low_back(values))

def matmul_high(left_operand, right_operand):
    return jnp.einsum('xcn,nr->xcr', left_operand, right_operand, precision=exact_matmul_mode)

def matmul_high_t(left_operand, right_operand):
    return jnp.einsum('hjk,tk->hjt', left_operand, right_operand, precision=exact_matmul_mode)

def layer_norm(values, gain_row, bias_row):
    center = values - lax.optimization_barrier(jnp.mean(values, axis=-1, keepdims=True))
    spread = lax.optimization_barrier(jnp.mean(center * center, axis=-1, keepdims=True))
    return center * lax.rsqrt(spread + eps_norm) * gain_row + bias_row

def shifted(values):
    return jnp.concatenate([jnp.zeros_like(values[:, :1]), values[:, :-1]], axis=1)

def fading_memory_scan(acceptor_lines, entering_lookup_lines, entering_payload_lines, fading_exponent_log, reward_entries, piece_opening_memory):
    group_count_total = EMBED_BREADTH // CHANNEL_GROUP

    def by_blocks(array):
        return array.reshape(SEGS, SEG_LEN // BLOCK, BLOCK, group_count_total, CHANNEL_GROUP).transpose(1, 2, 0, 3, 4)
    group_reward_entries = reward_entries.reshape(group_count_total, CHANNEL_GROUP)

    def token_step(running_memory, member):
        acceptor_step, key_t, value_t, decay_t = member
        lookup_payload_dyad = key_t[..., :, None] * value_t[..., None, :]
        emitted_per_step = jnp.einsum('nsc,nsch->nsh', acceptor_step, running_memory + group_reward_entries[None, :, :, None] * lookup_payload_dyad, precision=exact_matmul_mode)
        return (jnp.exp(decay_t)[..., None] * running_memory + lookup_payload_dyad, emitted_per_step)

    def block_step(running_memory, members):
        return lax.scan(token_step, running_memory, members)
    final_state, output_rows = lax.scan(jax.checkpoint(block_step), piece_opening_memory, (by_blocks(acceptor_lines), by_blocks(entering_lookup_lines), by_blocks(entering_payload_lines), by_blocks(fading_exponent_log)))
    return output_rows.transpose(2, 0, 1, 3, 4).reshape(SEGS, SEG_LEN, EMBED_BREADTH)

def forward(tokens, tm_mats, low_rank, channel_parameters, cm_key, cm_value, cm_recept, piece_opening_memory):
    mix_width = 5 * MIX_RANK
    values = tokens.reshape(SEGS, SEG_LEN, EMBED_BREADTH)
    normed = layer_norm(values, channel_parameters[0], channel_parameters[1])
    difference = shifted(normed) - normed
    mixed_x = low(normed + difference * channel_parameters[2])
    mix_low = low(jnp.tanh(low_back(matmul_high(mixed_x, low_rank[0][:, :mix_width]))))
    mix_groups = mix_low.reshape(SEGS, SEG_LEN, 5, MIX_RANK)
    up_groups = low_rank[1][:, :mix_width].reshape(EMBED_BREADTH, 5, MIX_RANK)
    mixes = low_back(jnp.einsum('slgr,dgr->gsld', mix_groups, up_groups, precision=exact_matmul_mode))
    inputs_five = [low(normed + difference * (channel_parameters[3 + number] + mixes[number])) for number in range(5)]
    x_decay, x_key, x_value, x_recept, x_gate = inputs_five
    decay_low = low(jnp.tanh(low_back(matmul_high(x_decay, low_rank[0][:, mix_width:]))))
    log_rate = channel_parameters[8] + low_back(matmul_high_t(decay_low, low_rank[1][:, mix_width:]))
    fading_exponent_log = -jnp.exp(log_rate)
    acceptor_lines = both_ways(matmul_high(x_recept, tm_mats[0]))
    keys_all = both_ways(matmul_high(x_key, tm_mats[1]))
    values_all = both_ways(matmul_high(x_value, tm_mats[2]))
    gate_pre = low_back(matmul_high(x_gate, tm_mats[3]))
    weighted_kv_output = fading_memory_scan(acceptor_lines, keys_all, values_all, fading_exponent_log, channel_parameters[9], piece_opening_memory)
    grouped = weighted_kv_output.reshape(SEGS, SEG_LEN, EMBED_BREADTH // CHANNEL_GROUP, CHANNEL_GROUP)
    center = grouped - lax.optimization_barrier(jnp.mean(grouped, axis=-1, keepdims=True))
    spread = lax.optimization_barrier(jnp.mean(center * center, axis=-1, keepdims=True))
    group_normed = (center * lax.rsqrt(spread + eps_group)).reshape(SEGS, SEG_LEN, EMBED_BREADTH)
    gated = low((group_normed * channel_parameters[10] + channel_parameters[11]) * jax.nn.silu(gate_pre))
    residual = values + low_back(matmul_high(gated, tm_mats[4]))
    second = low(layer_norm(residual, channel_parameters[12], channel_parameters[13]))
    step_diff = shifted(second) - second
    key_mix = low(second + step_diff * channel_parameters[14])
    recept_mix = low(second + step_diff * channel_parameters[15])
    hidden = low(jnp.square(jax.nn.relu(low_back(matmul_high(key_mix, cm_key)))))
    kv_all = low_back(matmul_high(hidden, cm_value))
    gate_cm = jax.nn.sigmoid(low_back(matmul_high(recept_mix, cm_recept)))
    block_out = residual + low(gate_cm * kv_all)
    return block_out.reshape(TOKENS, EMBED_BREADTH)

def reference(tokens, tm_mats, low_rank, channel_parameters, piece_opening_memory, cm_key, cm_value, cm_recept, out_grad):

    def as_float(array):
        return array.astype(jnp.float32)

    def closed(tokens_f, mats_f, rank_f, vectors_f, key_f, value_f, recept_f):
        return forward(tokens_f, mats_f, rank_f, vectors_f, key_f, value_f, recept_f, piece_opening_memory)
    block_out, pullback = jax.vjp(closed, as_float(tokens), as_float(tm_mats), as_float(low_rank), channel_parameters, as_float(cm_key), as_float(cm_value), as_float(cm_recept))
    grads = pullback(as_float(out_grad))
    return (block_out.astype(jnp.bfloat16), grads[0], grads[1], grads[2], grads[3], grads[4], grads[5], grads[6])
```

```python
import functools
import jax
import jax.numpy as jnp
from jax import lax
from jax.experimental import pallas as pl
from jax.experimental.pallas import tpu as pltpu
from jax.sharding import PartitionSpec as P

F = jnp.float32
HB = jnp.bfloat16
G = 64
B = 16
LANES = 128
MIX_RANK = 32
EPS_N = 1e-05
EPS_G = 0.00064
FLOOR = -120.0


def mm(a, b):
    return jnp.dot(a, b, preferred_element_type=F)


def mm_nt(a, b):
    return lax.dot_general(a, b, (((1,), (1,)), ((), ())), preferred_element_type=F)


def mm_tn(a, b):
    return lax.dot_general(a, b, (((0,), (0,)), ((), ())), preferred_element_type=F)


def head_mask(dt):
    i = lax.broadcasted_iota(jnp.int32, (LANES, LANES), 0) // G
    j = lax.broadcasted_iota(jnp.int32, (LANES, LANES), 1) // G
    return (i == j).astype(dt)


def head_sum(x, ones):
    hi = x.astype(HB)
    lo = (x - hi.astype(F)).astype(HB)
    return mm(hi, ones) + mm(lo, ones)


def block_sums(d):
    row = lax.broadcasted_iota(jnp.int32, d.shape, 1)
    run = d
    for step in (1, 2, 4, 8):
        run = run + jnp.where(row >= step, pltpu.roll(run, step, 1), 0.0)
    return run


def pair_rows(s):
    if s < 7:
        return 0, 16
    return 8, 8


def pair_weight(excl, incl, s):
    first, rows = pair_rows(s)
    gap = excl[:, first : first + rows, :] - incl[:, s : s + 1, :]
    if s != 7:
        u = first + lax.broadcasted_iota(jnp.int32, gap.shape, 1)
        gap = jnp.where(u > s, gap, -1e30)
    return jnp.exp(gap)


def silu_parts(g):
    sig = 1.0 / (1.0 + jnp.exp(-g))
    return sig, g * sig


def fwd_body(groups, nb, r_ref, k_ref, v_ref, rate_ref, gp_ref, vec_ref, s0_ref,
             z_ref, y_ref, st_ref, state):
    @pl.when(pl.program_id(0) == 0)
    def _():
        state[...] = s0_ref[...]

    ones = head_mask(HB)
    keep = head_mask(F)
    rows = nb * B
    for g in range(groups):
        cols = slice(g * LANES, (g + 1) * LANES)

        def blocks(ref):
            return ref[:, cols].astype(F).reshape(nb, B, LANES)

        r, k, v = blocks(r_ref), blocks(k_ref), blocks(v_ref)
        decay = jnp.maximum(-jnp.exp(blocks(rate_ref)), FLOOR)
        bonus, gn_g, gn_b = (vec_ref[i : i + 1, cols] for i in range(3))
        incl = block_sums(decay)
        excl = incl - decay
        last = incl[:, B - 1 : B, :]
        rq = (r * jnp.exp(excl)).astype(HB)
        kk = (k * jnp.exp(last - incl)).astype(HB)
        whole = jnp.exp(last)
        vb = v.astype(HB)
        from_state = []
        st = state[g]
        for b in range(nb):
            stb = st.astype(HB)
            st_ref[b, g] = stb
            from_state.append(mm_nt(rq[b], stb))
            st = st * whole[b] + keep * mm_tn(vb[b], kk[b])
        state[g] = st
        bits = []
        for s in range(B - 1):
            first, n = pair_rows(s)
            e = pair_weight(excl, incl, s)
            bits.append((r[:, first : first + n, :] * k[:, s : s + 1, :] * e).astype(HB).reshape(nb * n, LANES))
        bits.append((r * k * bonus).astype(HB).reshape(rows, LANES))
        scores = mm(jnp.concatenate(bits, axis=0), ones)
        at = 0
        low = jnp.zeros((nb, 8, LANES), F)
        high = jnp.zeros((nb, 8, LANES), F)
        for s in range(B - 1):
            first, n = pair_rows(s)
            part = scores[at : at + nb * n].reshape(nb, n, LANES) * v[:, s : s + 1, :]
            at += nb * n
            if n == 16:
                low = low + part[:, :8]
                high = high + part[:, 8:]
            else:
                high = high + part
        own = scores[at : at + rows].reshape(nb, B, LANES) * v
        y = jnp.concatenate([low, high], axis=1) + own
        y = y.reshape(rows, LANES) + jnp.concatenate(from_state, axis=0)
        y_ref[:, cols] = y
        center = y - head_sum(y, ones) * (1.0 / G)
        spread = head_sum(center * center, ones) * (1.0 / G)
        normed = center * lax.rsqrt(spread + EPS_G)
        _, act = silu_parts(gp_ref[:, cols])
        z_ref[:, cols] = ((normed * gn_g + gn_b) * act).astype(HB)


def wkv_forward(r, k, v, rate, gp, vec, start, step_tokens=128):
    tokens, width = r.shape
    groups = width // LANES
    nb = step_tokens // B
    steps = tokens // step_tokens
    row = pl.BlockSpec((step_tokens, width), lambda i: (i, 0))
    full = lambda shape: pl.BlockSpec(shape, lambda i: (0,) * len(shape))
    return pl.pallas_call(
        functools.partial(fwd_body, groups, nb),
        grid=(steps,),
        in_specs=[row, row, row, row, row, full(vec.shape), full(start.shape)],
        out_specs=[row, row, pl.BlockSpec((nb, groups, LANES, LANES), lambda i: (i, 0, 0, 0))],
        out_shape=[
            jax.ShapeDtypeStruct((tokens, width), HB),
            jax.ShapeDtypeStruct((tokens, width), F),
            jax.ShapeDtypeStruct((tokens // B, groups, LANES, LANES), HB),
        ],
        scratch_shapes=[pltpu.VMEM((groups, LANES, LANES), F)],
        cost_estimate=pl.CostEstimate(flops=tokens * width * 1024, transcendentals=tokens * width * 16, bytes_accessed=tokens * width * 40),
        name="wkv_forward",
    )(r, k, v, rate, gp, vec, start)


def bwd_body(groups, nb, r_ref, k_ref, v_ref, rate_ref, gp_ref, y_ref, gz_ref, vec_ref, st_ref,
             gr_ref, gk_ref, gv_ref, gg_ref, gd_ref, sums_ref, adj):
    first_step = pl.program_id(0) == 0

    @pl.when(first_step)
    def _():
        adj[...] = jnp.zeros_like(adj)
        sums_ref[...] = jnp.zeros_like(sums_ref)

    ones = head_mask(HB)
    keep = head_mask(F)
    rows = nb * B
    cols_of = []
    for s in range(B - 1):
        first, n = pair_rows(s)
        cols_of.append((s, first, n))
    for g in range(groups):
        cols = slice(g * LANES, (g + 1) * LANES)

        def blocks(x):
            return x.astype(F).reshape(nb, B, LANES)

        r, k, v = blocks(r_ref[:, cols]), blocks(k_ref[:, cols]), blocks(v_ref[:, cols])
        raw = -jnp.exp(blocks(rate_ref[:, cols]))
        decay = jnp.maximum(raw, FLOOR)
        bonus, gn_g, gn_b = (vec_ref[i : i + 1, cols] for i in range(3))
        y, gp, gz = y_ref[:, cols], gp_ref[:, cols], gz_ref[:, cols]
        center = y - head_sum(y, ones) * (1.0 / G)
        spread = head_sum(center * center, ones) * (1.0 / G)
        inv = lax.rsqrt(spread + EPS_G)
        normed = center * inv
        sig, act = silu_parts(gp)
        gated = gz * act
        gg_ref[:, cols] = (gz * (normed * gn_g + gn_b) * sig * (1.0 + gp * (1.0 - sig))).astype(HB)
        sums_ref[2:3, cols] += jnp.sum(gated * normed, axis=0, keepdims=True)
        sums_ref[3:4, cols] += jnp.sum(gated, axis=0, keepdims=True)
        gn = gated * gn_g
        gy = inv * (gn - head_sum(gn, ones) * (1.0 / G) - normed * (head_sum(gn * normed, ones) * (1.0 / G)))
        gy = gy.reshape(nb, B, LANES)
        incl = block_sums(decay)
        excl = incl - decay
        last = incl[:, B - 1 : B, :]
        to_start = jnp.exp(excl)
        to_end = jnp.exp(last - incl)
        whole = jnp.exp(last)
        rq = (r * to_start).astype(HB)
        kk = (k * to_end).astype(HB)
        vb = v.astype(HB)
        gyb = gy.astype(HB)
        lt = adj[g]
        gr_state, gk_state, gv_state, crossing = [None] * nb, [None] * nb, [None] * nb, [None] * nb
        for b in reversed(range(nb)):
            ltb = lt.astype(HB)
            stb = st_ref[b, g]
            gr_state[b] = mm(gyb[b], stb)
            gk_state[b] = mm(vb[b], ltb)
            gv_state[b] = mm_nt(kk[b], ltb)
            crossing[b] = jnp.sum(lt * stb.astype(F), axis=0, keepdims=True) * whole[b]
            lt = lt * whole[b] + keep * mm_tn(gyb[b], rq[b])
        adj[g] = lt
        stack = lambda parts: jnp.concatenate(parts, axis=0).reshape(nb, B, LANES)
        gr_in = stack(gr_state) * to_start
        gk_out = stack(gk_state) * to_end
        gv = stack(gv_state)
        e_bits, m_bits, a_bits, w_cache = [], [], [], []
        for s, first, n in cols_of:
            e = pair_weight(excl, incl, s)
            w_cache.append(e)
            a_bits.append((r[:, first : first + n] * k[:, s : s + 1] * e).astype(HB).reshape(nb * n, LANES))
            m_bits.append((gy[:, first : first + n] * v[:, s : s + 1]).astype(HB).reshape(nb * n, LANES))
        a_bits.append((r * k * bonus).astype(HB).reshape(rows, LANES))
        m_bits.append((gy * v).astype(HB).reshape(rows, LANES))
        scores = mm(jnp.concatenate(a_bits, axis=0), ones)
        dots = mm(jnp.concatenate(m_bits, axis=0), ones)
        at = 0
        low = jnp.zeros((nb, 8, LANES), F)
        high = jnp.zeros((nb, 8, LANES), F)
        p1, p2, p3 = [], [], []
        for (s, first, n), e in zip(cols_of, w_cache):
            m = dots[at : at + nb * n].reshape(nb, n, LANES)
            a = scores[at : at + nb * n].reshape(nb, n, LANES)
            at += nb * n
            me = m * e
            part = me * k[:, s : s + 1]
            if n == 16:
                low = low + part[:, :8]
                high = high + part[:, 8:]
            else:
                high = high + part
            mer = me * r[:, first : first + n]
            p1.append(mer)
            p2.append(a * gy[:, first : first + n])
            p3.append(mer * k[:, s : s + 1])
        a_own = scores[at : at + rows].reshape(nb, B, LANES)
        m_own = dots[at : at + rows].reshape(nb, B, LANES)
        gr = gr_in + jnp.concatenate([low, high], axis=1) + m_own * bonus * k
        gr_ref[:, cols] = gr.reshape(rows, LANES).astype(HB)
        p3.append(gr_in * r)
        p3.append(gk_out * k)
        total = sum(n for _, _, n in cols_of)
        col_s = jnp.concatenate([jnp.full((B, n), s, jnp.int32) for s, _, n in cols_of], axis=1)
        t = lax.broadcasted_iota(jnp.int32, (B, total), 0)
        pick = (col_s == t).astype(HB)
        col_u = jnp.concatenate([first + lax.broadcasted_iota(jnp.int32, (B, n), 1) for _, first, n in cols_of], axis=1)
        around = ((col_s < t) & (col_u > t)).astype(HB)
        i = lax.broadcasted_iota(jnp.int32, (B, B), 0)
        j = lax.broadcasted_iota(jnp.int32, (B, B), 1)
        around = jnp.concatenate([around, (j > i).astype(HB), (j < i).astype(HB)], axis=1)
        gk_pairs, gv_pairs, gd = [], [], []
        for b in range(nb):
            gk_pairs.append(mm(pick, jnp.concatenate([p[b] for p in p1], axis=0).astype(HB)))
            gv_pairs.append(mm(pick, jnp.concatenate([p[b] for p in p2], axis=0).astype(HB)))
            gd.append(mm(around, jnp.concatenate([p[b] for p in p3], axis=0).astype(HB)) + crossing[b])
        gk = gk_out + stack(gk_pairs) + m_own * bonus * r
        gk_ref[:, cols] = gk.reshape(rows, LANES).astype(HB)
        gv = gv + stack(gv_pairs) + a_own * gy
        gv_ref[:, cols] = gv.reshape(rows, LANES).astype(HB)
        grate = (stack(gd) * raw).reshape(rows, LANES)
        gd_ref[:, cols] = grate.astype(HB)
        sums_ref[0:1, cols] += jnp.sum((m_own * r * k).reshape(rows, LANES), axis=0, keepdims=True)
        sums_ref[1:2, cols] += jnp.sum(grate, axis=0, keepdims=True)


def wkv_backward(r, k, v, rate, gp, y, gz, vec, states, step_tokens=128):
    tokens, width = r.shape
    groups = width // LANES
    nb = step_tokens // B
    steps = tokens // step_tokens
    row = pl.BlockSpec((step_tokens, width), lambda i: (steps - 1 - i, 0))
    full = lambda shape: pl.BlockSpec(shape, lambda i: (0,) * len(shape))
    low = jax.ShapeDtypeStruct((tokens, width), HB)
    return pl.pallas_call(
        functools.partial(bwd_body, groups, nb),
        grid=(steps,),
        in_specs=[row] * 7 + [full(vec.shape), pl.BlockSpec((nb, groups, LANES, LANES), lambda i: (steps - 1 - i, 0, 0, 0))],
        out_specs=[row] * 5 + [full((8, width))],
        out_shape=[low] * 5 + [jax.ShapeDtypeStruct((8, width), F)],
        scratch_shapes=[pltpu.VMEM((groups, LANES, LANES), F)],
        cost_estimate=pl.CostEstimate(flops=tokens * width * 4096, transcendentals=tokens * width * 20, bytes_accessed=tokens * width * 60),
        name="wkv_backward",
    )(r, k, v, rate, gp, y, gz, vec, states)


def ring_of(count):
    deep = 4 if count % 4 == 0 and count >= 8 else 1
    wide = count // deep
    if deep == 1 or wide == 1:
        return list(range(count))
    path = []
    for z in range(deep):
        xs = range(1, wide) if z % 2 == 0 else range(wide - 1, 0, -1)
        path += [z * wide + x for x in xs]
    return path + [z * wide for z in reversed(range(deep))]


def ring_tables():
    count = lax.axis_size("seq")
    path = ring_of(count)
    place = [path.index(i) for i in range(count)]
    here = jnp.array(place, jnp.int32)[lax.axis_index("seq")]
    right = [(path[i], path[(i + 1) % count]) for i in range(count)]
    left = [(b, a) for a, b in right]
    return count, jnp.array(path, jnp.int32), here, right, left


def gather_seq(part, dim):
    count, path, here, right, left = ring_tables()
    size = part.shape[dim]
    shape = list(part.shape)
    shape[dim] = size * count
    out = jnp.zeros(shape, part.dtype)

    def put(out, piece, away):
        owner = path[(here + away) % count]
        return lax.dynamic_update_slice_in_dim(out, piece, owner * size, dim)

    out = put(out, part, 0)
    going_right = going_left = part
    for step in range(1, count // 2 + 1):
        going_right = lax.ppermute(going_right, "seq", right)
        if step < count - count // 2:
            going_left = lax.ppermute(going_left, "seq", left)
            out = put(out, going_left, step)
        out = put(out, going_right, -step)
    return out


def scatter_seq(piece_of):
    count, path, here, right, left = ring_tables()
    far = count // 2
    near = count - 1 - far

    def term(away):
        return piece_of(path[(here + away) % count])

    going_right = going_left = None
    for step in range(far, 0, -1):
        going_right = term(step) if going_right is None else term(step) + going_right.astype(F)
        going_right = lax.ppermute(going_right.astype(HB), "seq", right)
        if step <= near:
            going_left = term(-step) if going_left is None else term(-step) + going_left.astype(F)
            going_left = lax.ppermute(going_left.astype(HB), "seq", left)
    return term(0) + going_right.astype(F) + going_left.astype(F)


def exchange_seq(value, split, join):
    return lax.all_to_all(value, "seq", split_axis=split, concat_axis=join, tiled=True)


def previous(rows):
    return jnp.concatenate([jnp.zeros_like(rows[:1]), rows[:-1]], axis=0)


def following(rows):
    return jnp.concatenate([rows[1:], jnp.zeros_like(rows[:1])], axis=0)


def normalize(values):
    center = values - jnp.mean(values, axis=-1, keepdims=True)
    inverse = lax.rsqrt(jnp.mean(center * center, axis=-1, keepdims=True) + EPS_N)
    return center * inverse, inverse


def normalize_back(grad, normed, inverse, gain):
    scaled = grad * gain
    return inverse * (
        scaled
        - jnp.mean(scaled, axis=-1, keepdims=True)
        - normed * jnp.mean(scaled * normed, axis=-1, keepdims=True)
    )


def shards(tokens, tm_mats, low_rank, params, opening, cm_key, cm_value, cm_recept, out_grad):
    rows, width = tokens.shape
    count = lax.axis_size("seq")
    here = lax.axis_index("seq")
    total = rows * count
    cols = width // count
    mix_width = 5 * MIX_RANK
    g1, b1, mu_x = params[0], params[1], params[2]
    g2, b2, cmu_k, cmu_r = params[12], params[13], params[14], params[15]

    def my_cols(array):
        return lax.dynamic_slice_in_dim(array, here * cols, cols, array.ndim - 1)

    def my_rows(array):
        return lax.dynamic_slice_in_dim(array, here * rows, rows, 0)

    x = gather_seq(tokens, 0).astype(F)
    rank = lax.all_gather(low_rank, ("seg", "seq"), axis=1, tiled=True)
    mats = lax.all_gather(exchange_seq(tm_mats[:4], 2, 1), "seg", axis=1, tiled=True)
    w_output = lax.all_gather(tm_mats[4], ("seg", "seq"), axis=0, tiled=True)
    go_cols = exchange_seq(out_grad, 1, 0).astype(F)
    down_mix, down_decay = rank[0][:, :mix_width], rank[0][:, mix_width:]
    up_mix = rank[1][:, :mix_width]
    up_decay = lax.dynamic_slice_in_dim(rank[1], here * cols, cols, 0)[:, mix_width:]

    xhat, x_inv = normalize(x)
    xn = xhat * g1 + b1
    dx = previous(xn) - xn
    xm = (xn + dx * mu_x).astype(HB)
    m_f = jnp.tanh(mm(xm, down_mix))
    m = m_f.astype(HB)

    def group(array, j):
        return array[:, j * MIX_RANK : (j + 1) * MIX_RANK]

    lerp = [params[3 + j] + mm_nt(group(m, j), group(up_mix, j)) for j in range(5)]
    x_w, x_k, x_v, x_r, x_g = ((xn + dx * f).astype(HB) for f in lerp)
    e_f = jnp.tanh(mm(x_w, down_decay))
    e = e_f.astype(HB)
    rate = my_cols(params[8]) + mm_nt(e, up_decay)
    r = mm(x_r, mats[0]).astype(HB)
    k = mm(x_k, mats[1]).astype(HB)
    v = mm(x_v, mats[2]).astype(HB)
    gp = mm(x_g, mats[3])
    vec = my_cols(jnp.concatenate([params[9:12], jnp.zeros((5, width), F)], axis=0))
    groups = cols // LANES
    heads = lax.dynamic_slice_in_dim(opening[0], here * (cols // G), cols // G, 0)
    start = jnp.einsum(
        "ghkv,hi->ghvik", heads.reshape(groups, LANES // G, G, G), jnp.eye(LANES // G, dtype=F),
        precision=lax.Precision.HIGHEST,
    ).reshape(groups, LANES, LANES)
    z_cols, y, states = wkv_forward(r, k, v, rate, gp, vec, start)
    z = gather_seq(z_cols, 1)
    x1 = x + mm(z, w_output)

    x1hat, x1_inv = normalize(x1)
    xs = (x1hat * g2 + b2).astype(HB).astype(F)
    dxs = previous(xs) - xs
    ck = (xs + dxs * cmu_k).astype(HB)
    cr = (xs + dxs * cmu_r).astype(HB)
    sg = jax.nn.sigmoid(mm(cr, cm_recept))
    gkv = gather_seq((go_cols * sg).astype(HB), 1)
    hp = mm(ck, cm_key)
    hid = jnp.square(jax.nn.relu(hp)).astype(HB)
    kv = scatter_seq(lambda owner: mm(hid, lax.dynamic_slice_in_dim(cm_value, owner * cols, cols, 1)))
    cm_rows = exchange_seq((sg * kv).astype(HB), 0, 1)
    block_out = (my_rows(x1) + cm_rows.astype(F)).astype(HB)
    gsp = (go_cols * kv * sg * (1.0 - sg)).astype(HB)
    ghp = (mm_nt(gkv, cm_value) * (2.0 * jax.nn.relu(hp))).astype(HB)
    cm_value_grad = mm_tn(hid, gkv)
    cm_key_grad = mm_tn(ck, ghp)
    cm_recept_grad = mm_tn(cr, gsp)
    cm_grads = tuple(
        lax.psum(value.astype(HB), "seg").astype(F) for value in (cm_key_grad, cm_value_grad, cm_recept_grad)
    )
    gck = mm_nt(ghp, cm_key)
    gcr = mm_nt(gsp, cm_recept)
    d_cmu_k = jnp.sum(gck * dxs, axis=0)
    d_cmu_r = jnp.sum(gcr * dxs, axis=0)
    gxs_part = gck * (1.0 - cmu_k) + gcr * (1.0 - cmu_r) + following(gck * cmu_k + gcr * cmu_r)
    gxs = scatter_seq(lambda owner: lax.dynamic_slice_in_dim(gxs_part, owner * rows, rows, 0))
    own_hat, own_inv = my_rows(x1hat), my_rows(x1_inv)
    gx1 = out_grad.astype(F) + normalize_back(gxs, own_hat, own_inv, g2)
    d_g2 = jnp.sum(gxs * own_hat, axis=0)
    d_b2 = jnp.sum(gxs, axis=0)

    go1 = gather_seq(gx1.astype(HB), 0)
    gz = mm_nt(go1, lax.dynamic_slice_in_dim(w_output, here * cols, cols, 0))
    gr, gk, gv, ggp, grb, sums = wkv_backward(r, k, v, rate, gp, y, gz, vec, states)
    d_mats = jnp.stack(
        [mm_tn(a, b).astype(HB) for a, b in ((x_r, gr), (x_k, gk), (x_v, gv), (x_g, ggp), (z, my_cols(go1)))]
    )
    d_mats = lax.psum_scatter(d_mats, "seg", scatter_dimension=1, tiled=True)
    d_mats = exchange_seq(d_mats, 1, 2).astype(F)
    d_up_decay = mm_tn(grb, e)
    ge = (mm(grb, up_decay) * (1.0 - e_f * e_f)).astype(HB)
    d_down_decay = mm_tn(x_w, ge)
    gx = [
        mm_nt(ge, down_decay),
        mm_nt(gk, mats[1]),
        mm_nt(gv, mats[2]),
        mm_nt(gr, mats[0]),
        mm_nt(ggp, mats[3]),
    ]
    gdx = gx[0] * lerp[0] + gx[1] * lerp[1] + gx[2] * lerp[2] + gx[3] * lerp[3] + gx[4] * lerp[4]
    gmix = [a * dx for a in gx]
    d_mu = [jnp.sum(a, axis=0) for a in gmix]
    gmix = [a.astype(HB) for a in gmix]
    d_up_mix = jnp.concatenate([mm_tn(a, group(m, j)) for j, a in enumerate(gmix)], axis=1)
    gm = jnp.concatenate([mm(a, group(up_mix, j)) for j, a in enumerate(gmix)], axis=1)
    gm = (gm * (1.0 - m_f * m_f)).astype(HB)
    d_down_mix = mm_tn(xm, gm)
    gxm = mm_nt(gm, down_mix)
    d_mu_x = jnp.sum(gxm * dx, axis=0)
    gdx = gdx + gxm * mu_x
    gxn_part = gx[0] + gx[1] + gx[2] + gx[3] + gx[4] + gxm - gdx + following(gdx)
    gxn = scatter_seq(lambda owner: lax.dynamic_slice_in_dim(gxn_part, owner * rows, rows, 0))
    own_hat, own_inv = my_rows(xhat), my_rows(x_inv)
    input_grad = gx1 + normalize_back(gxn, own_hat, own_inv, g1)
    d_g1 = jnp.sum(gxn * own_hat, axis=0)
    d_b1 = jnp.sum(gxn, axis=0)

    def spread_out(array, dim):
        shape = list(array.shape)
        shape[dim] = width
        return lax.dynamic_update_slice_in_dim(jnp.zeros(shape, F), array, here * cols, dim)

    of_heads = spread_out(sums, 1)
    vectors = jnp.stack(
        [d_g1, d_b1, d_mu_x, *d_mu, of_heads[1], of_heads[0], of_heads[2], of_heads[3], d_g2, d_b2, d_cmu_k, d_cmu_r]
    )
    packed = jnp.concatenate(
        [d_down_mix, d_down_decay, d_up_mix, spread_out(d_up_decay, 0), vectors.T, jnp.zeros((width, 48), F)], axis=1
    )
    packed = lax.psum_scatter(packed, ("seg", "seq"), scatter_dimension=0, tiled=True)
    half = low_rank.shape[2]
    rank_grad = jnp.stack([packed[:, :half], packed[:, half : 2 * half]])
    vectors_grad = packed[:, 2 * half : 2 * half + 16].T
    return (block_out, input_grad, d_mats, rank_grad, vectors_grad, *cm_grads)


def solution(mesh):
    by_token = P(("seg", "seq"), None)
    in_specs = (
        by_token,
        P(None, ("seg", "seq"), None),
        P(None, ("seg", "seq"), None),
        P(),
        P("seg", None, None, None),
        P(None, "seq"),
        P("seq", None),
        P(None, "seq"),
        by_token,
    )
    out_specs = (
        by_token,
        by_token,
        P(None, ("seg", "seq"), None),
        P(None, ("seg", "seq"), None),
        P(None, ("seg", "seq")),
        P(None, "seq"),
        P("seq", None),
        P(None, "seq"),
    )
    return jax.shard_map(shards, mesh=mesh, in_specs=in_specs, out_specs=out_specs, check_vma=False)
```

```python
import functools
import jax
import jax.numpy as jnp
import numpy as np
from jax import lax
from jax.experimental import pallas as pl
from jax.experimental.pallas import tpu as pltpu
from jax.sharding import PartitionSpec as P

F = jnp.float32
HB = jnp.bfloat16
G = 64
B = 16
LANES = 128
MIX_RANK = 32
EPS_N = 1e-05
EPS_G = 0.00064
VMEM = 60 << 20
PAD = 256
FLOOR = -120.0


def mm(a, b):
    return jnp.dot(a, b, preferred_element_type=F)


def mm_nt(a, b):
    return lax.dot_general(a, b, (((1,), (1,)), ((), ())), preferred_element_type=F)


def mm_tn(a, b):
    return lax.dot_general(a, b, (((0,), (0,)), ((), ())), preferred_element_type=F)


def head_mask(dt):
    i = lax.broadcasted_iota(jnp.int32, (LANES, LANES), 0) // G
    j = lax.broadcasted_iota(jnp.int32, (LANES, LANES), 1) // G
    return (i == j).astype(dt)


def head_sum(x, ones):
    hi = x.astype(HB)
    lo = (x - hi.astype(F)).astype(HB)
    return mm(hi, ones) + mm(lo, ones)


def block_sums(d):
    row = lax.broadcasted_iota(jnp.int32, d.shape, 1)
    run = d
    for step in (1, 2, 4, 8):
        run = run + jnp.where(row >= step, pltpu.roll(run, step, 1), 0.0)
    return run


def pair_rows(s):
    if s < 7:
        return 0, 16
    return 8, 8


def pair_weight(excl, incl, s):
    first, rows = pair_rows(s)
    gap = excl[:, first : first + rows, :] - incl[:, s : s + 1, :]
    if s != 7:
        u = first + lax.broadcasted_iota(jnp.int32, gap.shape, 1)
        gap = jnp.where(u > s, gap, -1e30)
    return jnp.exp(gap)


def silu_parts(g):
    sig = 1.0 / (1.0 + jnp.exp(-g))
    return sig, g * sig


def fwd_body(groups, nb, r_ref, k_ref, v_ref, rate_ref, gp_ref, vec_ref, s0_ref,
             z_ref, y_ref, st_ref, state):
    @pl.when(pl.program_id(0) == 0)
    def _():
        state[...] = s0_ref[...]

    ones = head_mask(HB)
    keep = head_mask(F)
    rows = nb * B
    for g in range(groups):
        cols = slice(g * LANES, (g + 1) * LANES)

        def blocks(ref):
            return ref[:, cols].astype(F).reshape(nb, B, LANES)

        r, k, v = blocks(r_ref), blocks(k_ref), blocks(v_ref)
        decay = jnp.maximum(-jnp.exp(blocks(rate_ref)), FLOOR)
        bonus, gn_g, gn_b = (vec_ref[i : i + 1, cols] for i in range(3))
        incl = block_sums(decay)
        excl = incl - decay
        last = incl[:, B - 1 : B, :]
        rq = (r * jnp.exp(excl)).astype(HB)
        kk = (k * jnp.exp(last - incl)).astype(HB)
        whole = jnp.exp(last)
        vb = v.astype(HB)
        from_state = []
        st = state[g]
        for b in range(nb):
            stb = st.astype(HB)
            st_ref[b, g] = stb
            from_state.append(mm_nt(rq[b], stb))
            st = st * whole[b] + keep * mm_tn(vb[b], kk[b])
        state[g] = st
        bits = []
        for s in range(B - 1):
            first, n = pair_rows(s)
            e = pair_weight(excl, incl, s)
            bits.append((r[:, first : first + n, :] * k[:, s : s + 1, :] * e).astype(HB).reshape(nb * n, LANES))
        bits.append((r * k * bonus).astype(HB).reshape(rows, LANES))
        scores = mm(jnp.concatenate(bits, axis=0), ones)
        at = 0
        low = jnp.zeros((nb, 8, LANES), F)
        high = jnp.zeros((nb, 8, LANES), F)
        for s in range(B - 1):
            first, n = pair_rows(s)
            part = scores[at : at + nb * n].reshape(nb, n, LANES) * v[:, s : s + 1, :]
            at += nb * n
            if n == 16:
                low = low + part[:, :8]
                high = high + part[:, 8:]
            else:
                high = high + part
        own = scores[at : at + rows].reshape(nb, B, LANES) * v
        y = jnp.concatenate([low, high], axis=1) + own
        y = y.reshape(rows, LANES) + jnp.concatenate(from_state, axis=0)
        y_ref[:, cols] = y
        center = y - head_sum(y, ones) * (1.0 / G)
        spread = head_sum(center * center, ones) * (1.0 / G)
        normed = center * lax.rsqrt(spread + EPS_G)
        _, act = silu_parts(gp_ref[:, cols])
        z_ref[:, cols] = ((normed * gn_g + gn_b) * act).astype(HB)


def wkv_forward(r, k, v, rate, gp, vec, start, step_tokens=128):
    tokens, width = r.shape
    groups = width // LANES
    nb = step_tokens // B
    steps = tokens // step_tokens
    row = pl.BlockSpec((step_tokens, width), lambda i: (i, 0))
    full = lambda shape: pl.BlockSpec(shape, lambda i: (0,) * len(shape))
    return pl.pallas_call(
        functools.partial(fwd_body, groups, nb),
        grid=(steps,),
        in_specs=[row, row, row, row, row, full(vec.shape), full(start.shape)],
        out_specs=[row, row, pl.BlockSpec((nb, groups, LANES, LANES), lambda i: (i, 0, 0, 0))],
        out_shape=[
            jax.ShapeDtypeStruct((tokens, width), HB),
            jax.ShapeDtypeStruct((tokens, width), F),
            jax.ShapeDtypeStruct((tokens // B, groups, LANES, LANES), HB),
        ],
        scratch_shapes=[pltpu.VMEM((groups, LANES, LANES), F)],
        cost_estimate=pl.CostEstimate(flops=tokens * width * 1024, transcendentals=tokens * width * 16, bytes_accessed=tokens * width * 40),
        name="wkv_forward",
    )(r, k, v, rate, gp, vec, start)


def bwd_body(groups, nb, r_ref, k_ref, v_ref, rate_ref, gp_ref, y_ref, gz_ref, vec_ref, st_ref, adj_in, sums_in, *rest):
    gr_ref, gk_ref, gv_ref, gg_ref, gd_ref, adj, sums_ref = rest[-7:]

    @pl.when(pl.program_id(0) == 0)
    def _():
        adj[...] = adj_in[...]
        sums_ref[...] = sums_in[...]

    ones = head_mask(HB)
    keep = head_mask(F)
    rows = nb * B
    cols_of = []
    for s in range(B - 1):
        first, n = pair_rows(s)
        cols_of.append((s, first, n))
    for g in range(groups):
        cols = slice(g * LANES, (g + 1) * LANES)

        def blocks(x):
            return x.astype(F).reshape(nb, B, LANES)

        r, k, v = blocks(r_ref[:, cols]), blocks(k_ref[:, cols]), blocks(v_ref[:, cols])
        raw = -jnp.exp(blocks(rate_ref[:, cols]))
        decay = jnp.maximum(raw, FLOOR)
        bonus, gn_g, gn_b = (vec_ref[i : i + 1, cols] for i in range(3))
        y, gp, gz = y_ref[:, cols], gp_ref[:, cols], gz_ref[:, cols]
        center = y - head_sum(y, ones) * (1.0 / G)
        spread = head_sum(center * center, ones) * (1.0 / G)
        inv = lax.rsqrt(spread + EPS_G)
        normed = center * inv
        sig, act = silu_parts(gp)
        gated = gz * act
        gg_ref[:, cols] = (gz * (normed * gn_g + gn_b) * sig * (1.0 + gp * (1.0 - sig))).astype(HB)
        sums_ref[2:3, cols] += jnp.sum(gated * normed, axis=0, keepdims=True)
        sums_ref[3:4, cols] += jnp.sum(gated, axis=0, keepdims=True)
        gn = gated * gn_g
        gy = inv * (gn - head_sum(gn, ones) * (1.0 / G) - normed * (head_sum(gn * normed, ones) * (1.0 / G)))
        gy = gy.reshape(nb, B, LANES)
        incl = block_sums(decay)
        excl = incl - decay
        last = incl[:, B - 1 : B, :]
        to_start = jnp.exp(excl)
        to_end = jnp.exp(last - incl)
        whole = jnp.exp(last)
        rq = (r * to_start).astype(HB)
        kk = (k * to_end).astype(HB)
        vb = v.astype(HB)
        gyb = gy.astype(HB)
        lt = adj[g]
        gr_state, gk_state, gv_state, crossing = [None] * nb, [None] * nb, [None] * nb, [None] * nb
        for b in reversed(range(nb)):
            ltb = lt.astype(HB)
            stb = st_ref[b, g]
            gr_state[b] = mm(gyb[b], stb)
            gk_state[b] = mm(vb[b], ltb)
            gv_state[b] = mm_nt(kk[b], ltb)
            crossing[b] = jnp.sum(lt * stb.astype(F), axis=0, keepdims=True) * whole[b]
            lt = lt * whole[b] + keep * mm_tn(gyb[b], rq[b])
        adj[g] = lt
        stack = lambda parts: jnp.concatenate(parts, axis=0).reshape(nb, B, LANES)
        gr_in = stack(gr_state) * to_start
        gk_out = stack(gk_state) * to_end
        gv = stack(gv_state)
        e_bits, m_bits, a_bits, w_cache = [], [], [], []
        for s, first, n in cols_of:
            e = pair_weight(excl, incl, s)
            w_cache.append(e)
            a_bits.append((r[:, first : first + n] * k[:, s : s + 1] * e).astype(HB).reshape(nb * n, LANES))
            m_bits.append((gy[:, first : first + n] * v[:, s : s + 1]).astype(HB).reshape(nb * n, LANES))
        a_bits.append((r * k * bonus).astype(HB).reshape(rows, LANES))
        m_bits.append((gy * v).astype(HB).reshape(rows, LANES))
        scores = mm(jnp.concatenate(a_bits, axis=0), ones)
        dots = mm(jnp.concatenate(m_bits, axis=0), ones)
        at = 0
        low = jnp.zeros((nb, 8, LANES), F)
        high = jnp.zeros((nb, 8, LANES), F)
        p1, p2, p3 = [], [], []
        for (s, first, n), e in zip(cols_of, w_cache):
            m = dots[at : at + nb * n].reshape(nb, n, LANES)
            a = scores[at : at + nb * n].reshape(nb, n, LANES)
            at += nb * n
            me = m * e
            part = me * k[:, s : s + 1]
            if n == 16:
                low = low + part[:, :8]
                high = high + part[:, 8:]
            else:
                high = high + part
            mer = me * r[:, first : first + n]
            p1.append(mer)
            p2.append(a * gy[:, first : first + n])
            p3.append(mer * k[:, s : s + 1])
        a_own = scores[at : at + rows].reshape(nb, B, LANES)
        m_own = dots[at : at + rows].reshape(nb, B, LANES)
        gr = gr_in + jnp.concatenate([low, high], axis=1) + m_own * bonus * k
        gr_ref[:, cols] = gr.reshape(rows, LANES).astype(HB)
        p3.append(gr_in * r)
        p3.append(gk_out * k)
        total = sum(n for _, _, n in cols_of)
        col_s = jnp.concatenate([jnp.full((B, n), s, jnp.int32) for s, _, n in cols_of], axis=1)
        t = lax.broadcasted_iota(jnp.int32, (B, total), 0)
        pick = (col_s == t).astype(HB)
        col_u = jnp.concatenate([first + lax.broadcasted_iota(jnp.int32, (B, n), 1) for _, first, n in cols_of], axis=1)
        around = ((col_s < t) & (col_u > t)).astype(HB)
        i = lax.broadcasted_iota(jnp.int32, (B, B), 0)
        j = lax.broadcasted_iota(jnp.int32, (B, B), 1)
        around = jnp.concatenate([around, (j > i).astype(HB), (j < i).astype(HB)], axis=1)
        gk_pairs, gv_pairs, gd = [], [], []
        for b in range(nb):
            gk_pairs.append(mm(pick, jnp.concatenate([p[b] for p in p1], axis=0).astype(HB)))
            gv_pairs.append(mm(pick, jnp.concatenate([p[b] for p in p2], axis=0).astype(HB)))
            gd.append(mm(around, jnp.concatenate([p[b] for p in p3], axis=0).astype(HB)) + crossing[b])
        gk = gk_out + stack(gk_pairs) + m_own * bonus * r
        gk_ref[:, cols] = gk.reshape(rows, LANES).astype(HB)
        gv = gv + stack(gv_pairs) + a_own * gy
        gv_ref[:, cols] = gv.reshape(rows, LANES).astype(HB)
        grate = (stack(gd) * raw).reshape(rows, LANES)
        gd_ref[:, cols] = grate.astype(HB)
        sums_ref[0:1, cols] += jnp.sum((m_own * r * k).reshape(rows, LANES), axis=0, keepdims=True)
        sums_ref[1:2, cols] += jnp.sum(grate, axis=0, keepdims=True)


def wkv_backward(r, k, v, rate, gp, y, gz, vec, states, at, count, adj, sums, outs, step_tokens=128):
    tokens, width = r.shape
    groups = width // LANES
    nb = step_tokens // B
    steps = count // step_tokens
    full = lambda shape: pl.BlockSpec(shape, lambda i: (0,) * len(shape))
    low = jax.ShapeDtypeStruct((tokens, width), HB)
    top = at // step_tokens + steps - 1
    high = gz.shape[0] // step_tokens - 1 - (tokens - at - count) % gz.shape[0] // step_tokens
    row = pl.BlockSpec((step_tokens, width), lambda i: (top - i, 0))
    state = pl.BlockSpec((nb, groups, LANES, LANES), lambda i: (top - i, 0, 0, 0))
    *outs, adj, sums = pl.pallas_call(
        functools.partial(bwd_body, groups, nb),
        grid=(steps,),
        in_specs=[row] * 6 + [pl.BlockSpec((step_tokens, width), lambda i: (high - i, 0))]
        + [full(vec.shape), state, full(adj.shape), full(sums.shape)] + [pl.BlockSpec(memory_space=pl.ANY)] * len(outs),
        out_specs=[row] * 5 + [full(adj.shape), full(sums.shape)],
        out_shape=[low] * 5 + [jax.ShapeDtypeStruct(adj.shape, F), jax.ShapeDtypeStruct(sums.shape, F)],
        input_output_aliases={11 + i: i for i in range(len(outs))},
        cost_estimate=pl.CostEstimate(flops=count * width * 4096, transcendentals=count * width * 20, bytes_accessed=count * width * 60),
        name="wkv_backward",
    )(r, k, v, rate, gp, y, gz, vec, states, adj, sums, *outs)
    return outs, adj, sums


def normalize(values):
    center = values - jnp.mean(values, axis=-1, keepdims=True)
    inverse = lax.rsqrt(jnp.mean(center * center, axis=-1, keepdims=True) + EPS_N)
    return center * inverse, inverse


def normalize_back(grad, normed, inverse, gain):
    scaled = grad * gain
    return inverse * (
        scaled
        - jnp.mean(scaled, axis=-1, keepdims=True)
        - normed * jnp.mean(scaled * normed, axis=-1, keepdims=True)
    )


def shift_down(values, first_row):
    row = lax.broadcasted_iota(jnp.int32, values.shape, 0)
    return jnp.where(row == 0, first_row, pltpu.roll(values, 1, 0))


def shift_up(values, last_row):
    row = lax.broadcasted_iota(jnp.int32, values.shape, 0)
    count = values.shape[0]
    return jnp.where(row == count - 1, last_row, pltpu.roll(values, count - 1, 0))


def whole(array):
    return pl.BlockSpec(array.shape, lambda i: (0,) * array.ndim, pipeline_mode=pl.Buffered(1))


def lane_groups(shape):
    return lax.broadcasted_iota(jnp.int32, shape, 1) // MIX_RANK


def weight_cols(refs, slot):
    for ref in refs:
        yield ref[:, slot].reshape(ref.shape[0] * ref.shape[2], ref.shape[3])


def mix_forward_body(segs, x_ref, prm_ref, down_ref, up_ref, at_ref, *rest):
    w_refs = rest[:segs]
    r_ref, k_ref, v_ref, gp_ref, rate_ref, t_ref, xr_ref, xk_ref, xv_ref, xg_ref, last = rest[segs:]

    @pl.when(pl.program_id(0) == 0)
    def _():
        last[...] = jnp.zeros_like(last)

    prm = lambda i: prm_ref[i : i + 1, :]
    width, cols = x_ref.shape[1], r_ref.shape[1]
    normed, _ = normalize(x_ref[...].astype(F))
    xn = normed * prm(0) + prm(1)
    dx = shift_down(xn, last[0:1, :]) - xn
    last[0:1, :] = xn[xn.shape[0] - 1 :, :]
    t_mix = jnp.tanh(mm((xn + dx * prm(2)).astype(HB), down_ref[...]))
    group = lane_groups(t_mix.shape)
    low = t_mix.astype(HB)

    def mixed(j):
        own = jnp.where(group == j, low, jnp.zeros_like(low))
        return (xn + dx * (prm(3 + j) + mm_nt(own, up_ref[...]))).astype(HB)

    t_dec = jnp.tanh(mm(mixed(0), down_ref[...]))
    t_ref[...] = jnp.where(group < 5, t_mix, t_dec)
    dec = t_dec.astype(HB)
    own_cols = pl.ds(pl.multiple_of(at_ref[0], cols), cols)
    rate_ref[...] = prm_ref[8:9, own_cols] + mm_nt(jnp.where(group < 5, jnp.zeros_like(dec), dec), up_ref[own_cols, :])
    part = width // segs
    for j, slot, x_out, y_out in ((1, 1, xk_ref, k_ref), (2, 2, xv_ref, v_ref), (3, 0, xr_ref, r_ref), (4, 3, xg_ref, gp_ref)):
        x_out[...] = mixed(j)
        total = None
        for i, w in enumerate(weight_cols(w_refs, slot)):
            term = mm(x_out[:, pl.ds(pl.multiple_of(at_ref[1 + i], part), part)], w)
            total = term if total is None else total + term
        y_out[...] = total.astype(y_out.dtype)


def rank_halves(width):
    half = lambda h: pl.BlockSpec((width, PAD), lambda i, h=h: (0, h), pipeline_mode=pl.Buffered(1))
    return [half(0), half(1)]


SCALARS = pl.BlockSpec(memory_space=pltpu.SMEM)


def mix_forward(x, prm, rank, at, mats, tile=256):
    total, width = x.shape
    cols = mats[0].shape[3]
    row = lambda n: pl.BlockSpec((tile, n), lambda i: (i, 0))
    shape = lambda n, dt: jax.ShapeDtypeStruct((total, n), dt)
    return pl.pallas_call(
        functools.partial(mix_forward_body, len(mats)),
        grid=(total // tile,),
        in_specs=[row(width), whole(prm)] + rank_halves(width) + [SCALARS] + [whole(a) for a in mats],
        out_specs=[row(cols)] * 5 + [row(PAD)] + [row(width)] * 4,
        out_shape=[shape(cols, HB)] * 3 + [shape(cols, F)] * 2 + [shape(PAD, F)] + [shape(width, HB)] * 4,
        scratch_shapes=[pltpu.VMEM((8, width), F)],
        compiler_params=pltpu.CompilerParams(vmem_limit_bytes=VMEM),
        cost_estimate=pl.CostEstimate(flops=total * width * (8 * cols + 14 * 256), transcendentals=total * 512, bytes_accessed=total * width * 12),
        name="mix_forward",
    )(x, prm, rank, rank, at, *mats)


def residual_forward_body(pieces, x_ref, w_ref, prm_ref, recept_ref, go_ref, at_ref, *rest):
    z_refs = rest[: pieces + 1]
    x1_ref, ck_ref, cr_ref, sg_ref, gkv_ref, last = rest[pieces + 1 :]

    @pl.when(pl.program_id(0) == 0)
    def _():
        last[...] = jnp.zeros_like(last)

    prm = lambda i: prm_ref[i : i + 1, :]
    cols = recept_ref.shape[1]
    x1 = x_ref[...].astype(F)
    far = jnp.where(pl.program_id(0) < pl.num_programs(0) // 2, z_refs[pieces - 1][...], z_refs[pieces][...])
    for i, z in enumerate([ref[...] for ref in z_refs[: pieces - 1]] + [far]):
        x1 = x1 + mm(z, w_ref[pl.ds(pl.multiple_of(at_ref[i], cols), cols), :])
    x1_ref[...] = x1
    normed, _ = normalize(x1)
    xs = (normed * prm(12) + prm(13)).astype(HB).astype(F)
    dxs = shift_down(xs, last[0:1, :]) - xs
    last[0:1, :] = xs[xs.shape[0] - 1 :, :]
    ck_ref[...] = (xs + dxs * prm(14)).astype(HB)
    cr = (xs + dxs * prm(15)).astype(HB)
    cr_ref[...] = cr
    sg = 1.0 / (1.0 + jnp.exp(-mm(cr, recept_ref[...])))
    sg_ref[...] = sg
    gkv_ref[...] = (go_ref[...].astype(F) * sg).astype(HB)


def residual_forward(x, z, z_far, at, w_output, prm, recept, go_cols, tile=256):
    total, width = x.shape
    cols = recept.shape[1]
    half = total // tile // 2
    row = lambda n: pl.BlockSpec((tile, n), lambda i: (i, 0))
    shape = lambda n, dt: jax.ShapeDtypeStruct((total, n), dt)
    halves = [pl.BlockSpec((tile, cols), lambda i: (jnp.minimum(i, half - 1), 0)), pl.BlockSpec((tile, cols), lambda i: (jnp.maximum(i - half, 0), 0))]
    return pl.pallas_call(
        functools.partial(residual_forward_body, len(z) + 1),
        grid=(total // tile,),
        in_specs=[row(width), whole(w_output), whole(prm), whole(recept), row(cols), SCALARS] + [row(cols)] * len(z) + halves,
        out_specs=[row(width)] * 3 + [row(cols)] * 2,
        out_shape=[shape(width, F), shape(width, HB), shape(width, HB), shape(cols, F), shape(cols, HB)],
        scratch_shapes=[pltpu.VMEM((8, width), F)],
        compiler_params=pltpu.CompilerParams(vmem_limit_bytes=VMEM),
        cost_estimate=pl.CostEstimate(flops=2 * total * width * (width + cols), transcendentals=total * cols, bytes_accessed=total * width * 12),
        name="residual_forward",
    )(x, w_output, prm, recept, go_cols, at, *z, *z_far)


def residual_backward_body(closes, x1_ref, before_ref, go_ref, ghp_ref, gsp_ref, key_ref, recept_ref, w_ref, prm_ref,
                           sums_in, ahead_in, *rest):
    gx1_ref, gz_ref, sums_ref, ahead = rest[-4:]
    at = pl.program_id(0)

    @pl.when(at == 0)
    def _():
        ahead[...] = ahead_in[...]
        sums_ref[...] = sums_in[...]

    prm = lambda i: prm_ref[i : i + 1, :]
    normed, inverse = normalize(x1_ref[...])
    xs = (normed * prm(12) + prm(13)).astype(HB).astype(F)
    other, _ = normalize(before_ref[...])
    other = (other[7:8, :] * prm(12) + prm(13)).astype(HB).astype(F)
    if closes:
        other = jnp.where(at == pl.num_programs(0) - 1, 0.0, other)
    dxs = shift_down(xs, other) - xs
    gck = mm_nt(ghp_ref[...], key_ref[...])
    gcr = mm_nt(gsp_ref[...], recept_ref[...])
    moved = gck * prm(14) + gcr * prm(15)
    gxs = gck + gcr - moved + shift_up(moved, ahead[0:1, :])
    ahead[0:1, :] = moved[0:1, :]
    total = lambda a: jnp.sum(a, axis=0, keepdims=True)
    sums_ref[0:1, :] += total(gxs * normed)
    sums_ref[1:2, :] += total(gxs)
    sums_ref[2:3, :] += total(gck * dxs)
    sums_ref[3:4, :] += total(gcr * dxs)
    gx1 = (go_ref[...].astype(F) + normalize_back(gxs, normed, inverse, prm(12))).astype(HB)
    gx1_ref[...] = gx1
    gz_ref[...] = mm_nt(gx1, w_ref[...]).astype(HB)


def residual_backward(x1, go_own, ghp, gsp, key, recept, w_output, prm, part, parts, sums, ahead, tile=256):
    total, width = x1.shape
    steps = total // tile // parts
    top = total // tile - 1 - part * steps
    row = lambda n: pl.BlockSpec((tile, n), lambda i: (top - i, 0))
    to = lambda n: pl.BlockSpec((tile, n), lambda i: (steps - 1 - i, 0))
    before = pl.BlockSpec((8, width), lambda i: (jnp.maximum((top - i) * (tile // 8) - 1, 0), 0))
    low = jax.ShapeDtypeStruct((total // parts, width), HB)
    few = jax.ShapeDtypeStruct((8, width), F)
    const = pl.BlockSpec((8, width), lambda i: (0, 0))
    flops = steps * tile * width * 2 * (width + ghp.shape[1] + gsp.shape[1])
    return pl.pallas_call(
        functools.partial(residual_backward_body, part == parts - 1),
        grid=(steps,),
        in_specs=[row(width), before, row(width), row(ghp.shape[1]), row(gsp.shape[1])] + [whole(a) for a in (key, recept, w_output, prm)] + [const, const],
        out_specs=[to(width), to(width), const, const],
        out_shape=[low, low, few, few],
        compiler_params=pltpu.CompilerParams(vmem_limit_bytes=VMEM),
        cost_estimate=pl.CostEstimate(flops=flops, transcendentals=total, bytes_accessed=steps * tile * width * 12),
        name="residual_backward",
    )(x1, x1, go_own, ghp, gsp, key, recept, w_output, prm, sums, ahead)


def mix_backward_body(opens, closes, segs, x_ref, before_ref, gr_ref, gk_ref, gv_ref, gg_ref, grb_ref, t_ref, gx1_ref,
                      prm_ref, two_ref, heads_ref, down_ref, up_ref, at_ref, *rest):
    w_refs, rest = rest[:segs], rest[segs:]
    given = rest[: 0 if opens else 3]
    out_ref, ahead, packed, *more = rest[len(given) :]
    gmix, mstack, gx_ref = more[-3:]
    at = pl.program_id(0)
    width, cols = x_ref.shape[1], gr_ref.shape[1]
    part = width // segs
    tile = x_ref.shape[0]

    @pl.when(at == 0)
    def _():
        if opens:
            ahead[...] = jnp.zeros_like(ahead)
            packed[...] = jnp.zeros_like(packed)
        else:
            ahead[...] = given[1][...]
            packed[...] = given[2][...]

    own_cols = pl.ds(pl.multiple_of(at_ref[0], cols), cols)
    prm = lambda i: prm_ref[i : i + 1, :]
    normed, inverse = normalize(x_ref[...].astype(F))
    xn = normed * prm(0) + prm(1)
    other, _ = normalize(before_ref[...].astype(F))
    other = other[15:16, :] * prm(0) + prm(1)
    if closes:
        first_tile = at == pl.num_programs(0) - 1
        other = jnp.where(first_tile, 0.0, other)
    dx = shift_down(xn, other) - xn
    t = t_ref[...]
    slope = 1.0 - t * t
    low = t.astype(HB)
    group = lane_groups(t.shape)
    lane = lax.broadcasted_iota(jnp.int32, t.shape, 1)
    zero = jnp.zeros_like(low)
    dec = jnp.where((group < 5) | (group == 7), zero, low)
    ge = jnp.where(group < 5, 0.0, mm(grb_ref[...], up_ref[own_cols, :]) * slope).astype(HB)
    packed[PAD : 2 * PAD, own_cols] += mm_tn(dec, grb_ref[...])
    gdx = gsum = gm = None
    for j, (slot, g_ref) in enumerate(((None, None), (1, gk_ref), (2, gv_ref), (0, gr_ref), (3, gg_ref))):
        own = jnp.where(group == j, low, zero)
        mstack[j * tile : (j + 1) * tile, :] = jnp.where(lane == 7 * MIX_RANK + j, jnp.ones_like(own), own)
        lerp = prm(3 + j) + mm_nt(own, up_ref[...])
        if j == 0:
            gx = mm_nt(ge, down_ref[...])
            x_w = (xn + dx * lerp).astype(HB)
        else:
            for i, w in enumerate(weight_cols(w_refs, slot)):
                gx_ref[:, pl.ds(pl.multiple_of(at_ref[1 + i], part), part)] = mm_nt(g_ref[...], w)
            gx = gx_ref[...]
        moved = gx * lerp
        gdx = moved if gdx is None else gdx + moved
        gsum = gx if gsum is None else gsum + gx
        bits = (gx * dx).astype(HB)
        gmix[j * tile : (j + 1) * tile, :] = bits
        part_m = jnp.where(group == j, mm(bits, up_ref[...]), 0.0)
        gm = part_m if gm is None else gm + part_m
    gm = (gm * slope).astype(HB)
    gxm = mm_nt(gm, down_ref[...])
    gdx = gdx + gxm * prm(2)
    gxn = gsum + gxm - gdx + shift_up(gdx, ahead[0:1, :])
    ahead[0:1, :] = gdx[0:1, :]
    total = lambda a: jnp.sum(a, axis=0, keepdims=True)
    xm = (xn + dx * prm(2)).astype(HB)
    packed[:PAD, :] += mm_tn(jnp.concatenate([gm, ge], axis=0), jnp.concatenate([xm, x_w], axis=0))
    packed[PAD : 2 * PAD, :] += mm_tn(mstack[...], gmix[...])
    spare = 7 * MIX_RANK
    packed[spare : spare + 1, :] += total(gxn * normed)
    packed[spare + 1 : spare + 2, :] += total(gxn)
    packed[spare + 2 : spare + 3, :] += total(gxm * dx)
    out_ref[...] = (gx1_ref[...].astype(F) + normalize_back(gxn, normed, inverse, prm(0))).astype(HB)
    if closes:
        @pl.when(first_tile)
        def _():
            packed[spare + 8 : spare + 16, :] += two_ref[...]
            packed[spare + 16 : spare + 24, own_cols] += heads_ref[...]
            block = more[0].shape[2]
            for i in range(more[0].shape[0]):
                more[0][i] = packed[:, i * block : (i + 1) * block].astype(HB)


def mix_backward(x, grads, t, gx1_parts, mats, rank, prm, two, heads, at, first_tile, steps, given, tile=256):
    total, width = x.shape
    segs = len(mats)
    cols = mats[0].shape[3]
    lines = 2 * PAD
    shape = jax.ShapeDtypeStruct
    fixed = lambda *s: pl.BlockSpec(s, lambda i: (0,) * len(s))
    top = first_tile
    row = lambda n: pl.BlockSpec((tile, n), lambda i: (top - i, 0))
    per = total // tile // len(gx1_parts)
    first = top // per * per
    gx1 = gx1_parts[len(gx1_parts) - 1 - top // per]
    before = pl.BlockSpec((16, width), lambda i: (jnp.maximum((top - i) * (tile // 16) - 1, 0), 0))
    closes = top - steps < 0
    return pl.pallas_call(
        functools.partial(mix_backward_body, not given, closes, segs),
        grid=(steps,),
        in_specs=[row(width), before] + [row(cols)] * 5 + [row(PAD), pl.BlockSpec((tile, width), lambda i: (top - first - i, 0))]
        + [whole(a) for a in (prm, two, heads)] + rank_halves(width) + [SCALARS] + [whole(a) for a in mats]
        + ([pl.BlockSpec(memory_space=pl.ANY), whole(given[1]), whole(given[2])] if given else []),
        out_specs=[row(width), fixed(8, width), fixed(lines, width)] + [fixed(segs, lines, width // segs)] * closes,
        out_shape=[shape((total, width), HB), shape((8, width), F), shape((lines, width), F)] + [shape((segs, lines, width // segs), HB)] * closes,
        input_output_aliases={15 + segs: 0} if given else {},
        scratch_shapes=[pltpu.VMEM((5 * tile, width), HB), pltpu.VMEM((5 * tile, PAD), HB), pltpu.VMEM((tile, width), F)],
        compiler_params=pltpu.CompilerParams(vmem_limit_bytes=VMEM),
        cost_estimate=pl.CostEstimate(flops=steps * tile * width * (8 * cols + 26 * 256), transcendentals=total, bytes_accessed=steps * tile * width * 10),
        name="mix_backward",
    )(x, x, *grads, t, gx1, prm, two, heads, rank, rank, at, *mats, *given)


def ring_of(count):
    deep = 4 if count % 4 == 0 and count >= 8 else 1
    wide = count // deep
    if deep == 1 or wide == 1:
        return list(range(count))
    path = []
    for z in range(deep):
        xs = range(1, wide) if z % 2 == 0 else range(wide - 1, 0, -1)
        path += [z * wide + x for x in xs]
    return path + [z * wide for z in reversed(range(deep))]


class Ring:
    def __init__(self, scale=1):
        self.count = lax.axis_size("seq")
        self.path = ring_of(self.count)
        place = [self.path.index(i) for i in range(self.count)]
        table = [[self.path[(place[i] + away) % self.count] for away in range(self.count)] for i in range(self.count)]
        self.scale = np.uint32(scale)
        here = lax.axis_index("seq").astype(jnp.uint32)
        self.row = lax.dynamic_slice(np.array(table, np.uint32), (here, np.uint32(0)), (1, self.count))
        self.right = [(self.path[i], self.path[(i + 1) % self.count]) for i in range(self.count)]
        self.left = [(b, a) for a, b in self.right]

    def owner(self, away):
        away %= self.count
        index = lax.reshape(lax.slice(self.row, (0, away), (1, away + 1)), ())
        return index * self.scale if self.scale > 1 else index


def starts(ndim, at):
    return [at.get(d, np.uint32(0)) for d in range(ndim)]


def cut(array, start, size, dim):
    sizes = list(array.shape)
    sizes[dim] = size
    return lax.dynamic_slice(array, starts(array.ndim, {dim: start}), sizes)


def put(array, piece, at):
    return lax.dynamic_update_slice(array, piece, starts(array.ndim, at))


def ring_hops(part, other=None):
    ring = Ring()
    half = part.shape[0] // 2
    held = [(0, part)]
    going_right = going_left = part
    for step in range(1, ring.count // 2):
        going_right = lax.ppermute(going_right, "seq", ring.right)
        going_left = lax.ppermute(going_left, "seq", ring.left)
        if step == 1 and other is not None:
            going_right, going_left = after((going_right, going_left), other)
        held += [(-step, going_right), (step, going_left)]
    far = lax.ppermute(going_right[:half], "seq", ring.right), lax.ppermute(going_left[half:], "seq", ring.left)
    return held, far


def assembled(held, far, dim):
    part = held[0][1]
    size = part.shape[dim]
    ring = Ring(size)
    shape = list(part.shape)
    shape[dim] = size * ring.count
    out = jnp.zeros(shape, part.dtype)
    for away, piece in held:
        out = put(out, piece, {dim: ring.owner(away)})
    half = part.shape[0] // 2
    start = ring.owner(ring.count // 2)
    out = put(out, far[0], {dim: start})
    low = {dim: start + np.uint32(half)} if dim == 0 else {dim: start, 0: np.uint32(half)}
    return put(out, far[1], low)


def gather_seq(part, dim, other=None):
    return assembled(*ring_hops(part, other), dim)


def after(value, other):
    return lax.optimization_barrier((value, other))[0]


class Scatter:
    def __init__(self, piece_of, scale):
        self.ring = Ring(scale)
        self.right, self.left = self.ring.right, self.ring.left
        self.piece_of = piece_of
        self.hops = self.step = self.ring.count // 2
        self.going = None

    def term(self, away):
        return self.piece_of(self.ring.owner(away))

    def hop(self, other=None):
        if self.going is None:
            last = self.term(self.hops)
            half = last.shape[0] // 2
            more, less = last[:half], last[half:]
        else:
            from_left, from_right = self.going if other is None else after(self.going, other)
            more, less = self.term(self.step), self.term(-self.step)
            if self.step == self.hops - 1:
                half = from_left.shape[0]
                more = jnp.concatenate([more[:half] + from_left.astype(F), more[half:]], axis=0)
                less = jnp.concatenate([less[:half], less[half:] + from_right.astype(F)], axis=0)
            else:
                more = more + from_left.astype(F)
                less = less + from_right.astype(F)
        sent = more.astype(HB), less.astype(HB)
        self.going = lax.ppermute(sent[0], "seq", self.right), lax.ppermute(sent[1], "seq", self.left)
        self.step -= 1
        return sent

    def finish(self, other=None):
        while self.step > 0:
            self.hop()
        from_left, from_right = self.going if other is None else after(self.going, other)
        return self.term(0) + from_left.astype(F) + from_right.astype(F)


def scatter_seq(piece_of, scale):
    return Scatter(piece_of, scale).finish()


def gather_seg(part):
    count = lax.axis_size("seg")
    held = {0: part}
    step = count // 2
    while step:
        pairs = [(i, i ^ step) for i in range(count)]
        held.update({i ^ step: lax.ppermute(value, "seg", pairs) for i, value in list(held.items())})
        step //= 2
    return [held[i] for i in range(count)]


def seg_bit(step):
    return (lax.axis_index("seg").astype(jnp.uint32) & np.uint32(step)) // np.uint32(step) if step > 1 else lax.axis_index("seg").astype(jnp.uint32) & np.uint32(1)


def seg_round(parts, step):
    count = lax.axis_size("seg")
    bit = seg_bit(step)
    shaped = parts.reshape((parts.shape[0] // 2, 2) + parts.shape[1:])
    keep = lax.squeeze(cut(shaped, bit, 1, 1), (1,))
    give = lax.squeeze(cut(shaped, np.uint32(1) - bit, 1, 1), (1,))
    return keep, lax.ppermute(give, "seg", [(i, i ^ step) for i in range(count)])


def scatter_seg(parts):
    step = 1
    while step < lax.axis_size("seg"):
        keep, come = seg_round(parts, step)
        parts = (keep.astype(F) + come.astype(F)).astype(HB)
        step *= 2
    return parts[0]


class Pump:
    def __init__(self, values):
        count = lax.axis_size("seg")
        self.values, self.done, self.coming = list(values), [], None
        self.rounds = [[(i, i ^ (2 << n)) for i in range(count)] for n in range((count // 2).bit_length() - 1)]

    def send(self):
        self.coming = lax.ppermute(self.values[len(self.done)], "seg", self.rounds[0])

    def turn(self, other):
        at = len(self.done)
        if self.coming is None and at < len(self.values):
            self.values[at] = after(self.values[at], other)
            self.send()
            return self.values[at]
        if at < len(self.values):
            value = self.values[at]
            value = (value.astype(F) + after(self.coming, other).astype(F)).astype(HB)
            for pairs in self.rounds[1:]:
                value = (value.astype(F) + lax.ppermute(value, "seg", pairs).astype(F)).astype(HB)
            self.done.append(value)
            if at + 1 < len(self.values):
                self.send()
            return value
        return other


def direct_exchange(array, cols):
    ring = Ring(cols)
    count, order = ring.count, ring.path
    entry = lambda away: cut(array, ring.owner(away), cols, array.ndim - 1)[None]
    senders = Ring()
    out = put(jnp.zeros((count,) + entry(0).shape[1:], array.dtype), entry(0), {0: senders.owner(0)})
    for away in sorted(range(1, count), key=lambda d: -min(d, count - d)):
        pairs = [(order[i], order[(i + away) % count]) for i in range(count)]
        out = put(out, lax.ppermute(entry(away), "seq", pairs), {0: senders.owner(-away)})
    return out


def exchange_seq(value, split, join):
    return lax.all_to_all(value, "seq", split_axis=split, concat_axis=join, tiled=True)


def shards(tokens, tm_mats, low_rank, params, opening, cm_key, cm_value, cm_recept, out_grad):
    rows, width = tokens.shape
    count = lax.axis_size("seq")
    segs = lax.axis_size("seg")
    here = lax.axis_index("seq").astype(jnp.uint32)
    total = rows * count
    cols = width // count
    ranks = low_rank.shape[2]
    first_row, first_col = here * np.uint32(rows), here * np.uint32(cols)

    def my_cols(array):
        return cut(array, first_col, cols, array.ndim - 1)

    def my_rows(array):
        return cut(array, first_row, rows, 0)

    low = jnp.pad(low_rank, ((0, 0), (0, 0), (0, PAD - ranks))).transpose(1, 0, 2).reshape(-1, 2 * PAD)
    rank = lax.all_gather(low, ("seg", "seq"), axis=0, tiled=True)
    mine = direct_exchange(tm_mats[:4], cols)
    mats = gather_seg(mine)
    x = gather_seq(tokens, 0, mine)
    w_output = lax.all_gather(after(tm_mats[4], x), ("seg", "seq"), axis=0, tiled=True)
    go_cols = exchange_seq(after(out_grad, x), 1, 0)
    part = width // segs
    seg_starts = [(lax.axis_index("seg") ^ i) * part for i in range(segs)]
    at = jnp.stack([first_col.astype(jnp.int32)] + seg_starts)

    r, k, v, gp, rate, t, x_r, x_k, x_v, x_g = mix_forward(x, params, rank, at, mats)
    vec = my_cols(jnp.concatenate([params[9:12], jnp.zeros((5, width), F)], axis=0))
    groups = cols // LANES
    heads = cut(opening[0], here * np.uint32(cols // G), cols // G, 0)
    start = jnp.einsum(
        "ghkv,hi->ghvik", heads.reshape(groups, LANES // G, G, G), jnp.eye(LANES // G, dtype=F),
        precision=lax.Precision.HIGHEST,
    ).reshape(groups, LANES, LANES)
    r, go_cols = lax.optimization_barrier((r, go_cols))
    z_cols, y, states = wkv_forward(r, k, v, rate, gp, vec, start)
    z_held, z_far = ring_hops(z_cols)
    ring_cols = Ring(cols)
    z_at = jnp.stack([ring_cols.owner(away).astype(jnp.int32) for away in [a for a, _ in z_held] + [count // 2]])

    x1, ck, cr, sg, gkv_cols = residual_forward(
        x, [piece for _, piece in z_held], z_far, z_at, w_output, params, cm_recept, go_cols
    )
    gkv = gather_seq(gkv_cols, 1)
    hp = mm(ck, cm_key)
    hid = jnp.square(jax.nn.relu(hp)).astype(HB)
    late = after(hid, gkv)
    kv = scatter_seq(lambda start: mm(late, cut(cm_value, start, cols, 1)), cols)
    cm_rows = exchange_seq((sg * kv).astype(HB), 0, 1)
    block_out = (my_rows(x1) + cm_rows.astype(F)).astype(HB)
    gsp = (go_cols.astype(F) * kv * sg * (1.0 - sg)).astype(HB)
    ghp = (mm_nt(gkv, cm_value) * (2.0 * jax.nn.relu(hp))).astype(HB)
    bit = seg_bit(1)
    near = [(i, i ^ 1) for i in range(segs)]

    def cm_half(which, ordered):
        part = lambda a: cut(a, which * np.uint32(a.shape[1] // 2), a.shape[1] // 2, 1)
        pairs = ((ck, ghp), (hid, gkv), (cr, gsp))
        return tuple(mm_tn(part(a), b).astype(HB) for a, b in pairs[ordered:])

    cm_come = tuple(lax.ppermute(value, "seg", near) for value in cm_half(np.uint32(1) - bit, 0))
    cm_kept = cm_half(bit, 0)
    gsp, ghp, cm_kept = lax.optimization_barrier((gsp, ghp, cm_kept))
    go_own = put(jnp.zeros((total, width), HB), out_grad, {0: first_row})

    def piece_cols(array):
        return lambda start: cut(array, start, cols, 1).astype(F)

    back = lambda part, *carried: residual_backward(
        x1, go_own, ghp, gsp, cm_key, cm_recept, w_output, params, part, 2, *carried
    )
    start_row = jnp.zeros((8, width), F)
    gx1_late, gz_late, sums_two, ahead = back(0, start_row, start_row)
    cm_kept = [(a.astype(F) + b.astype(F)).astype(HB) for a, b in zip(cm_kept, after(cm_come, ahead))]
    pump = Pump([a[i * (a.shape[0] // 2) : (i + 1) * (a.shape[0] // 2)] for a in cm_kept[:2] for i in range(2)] + cm_kept[2:])
    sent = pump.turn(ahead)
    late = Scatter(piece_cols(gz_late), cols)
    sent = (late.hop(), sent)
    gx1_early, gz_early, sums_two, ahead = back(1, sums_two, after(ahead, sent))
    token = pump.turn(gz_early)
    while late.step > 0:
        sent = late.hop((gz_early, sent))
    early = Scatter(piece_cols(gz_early), cols)
    gz_late = late.finish((sent, token))

    adj = jnp.zeros((groups, LANES, LANES), F)
    sums = jnp.zeros((8, cols), F)
    outs = ()
    half = total // 2
    runs = 2
    run = half // runs
    wkv = lambda gz, at, adj, sums, outs: wkv_backward(r, k, v, rate, gp, y, gz, vec, states, at, run, adj, sums, outs)
    sent = early.hop(None)
    for i in range(runs):
        outs, adj, sums = wkv(gz_late, total - (i + 1) * run, after(adj, sent), sums, outs)
        sent = pump.turn(sums)
        while early.step > early.hops * (runs - 1 - i) // runs:
            sent = (early.hop(sums), sent)
    gz_early = early.finish((sums, sent))
    go1 = Scatter(piece_cols(jnp.concatenate([gx1_early, gx1_late], axis=0)), cols)
    first_pieces = go1.piece_of
    go1.piece_of = lambda owner: after(first_pieces(owner), gz_early)
    sent = go1.hop()
    for i in range(runs):
        outs, adj, sums = wkv(gz_early, half - (i + 1) * run, after(adj, sent), sums, outs)
        sent = (go1.hop(sums), pump.turn(sums))
    gr, gk, gv, ggp, grb = outs
    d_four = jnp.stack([mm_tn(a, b).astype(HB) for a, b in ((x_r, gr), (x_k, gk), (x_v, gv), (x_g, ggp))], axis=1)
    keep, come = seg_round(d_four.reshape(segs, -1, 4, cols), 1)
    tiles = total // 256
    splits = (tiles // 4, tiles // 4, tiles // 2)

    def mix(run, grad, given):
        return mix_backward(
            x, (grad, gk, gv, ggp, grb), t, (gx1_late, gx1_early), mats, rank, params, sums_two, sums,
            at, tiles - 1 - sum(splits[:run]), splits[run], given,
        )

    def seg_rest(keep, come, step):
        parts = (keep.astype(F) + come.astype(F)).astype(HB)
        while step * 2 < segs:
            step *= 2
            keep, come = seg_round(parts, step)
            parts = (keep.astype(F) + come.astype(F)).astype(HB)
        return parts[0]

    d_four = (keep.astype(F) + come.astype(F)).astype(HB)
    keep, come = seg_round(d_four, 2)
    gr, _ = lax.optimization_barrier((gr, (sent, keep)))
    out, ahead, packed = mix(0, gr, ())
    while go1.step > 0:
        sent = go1.hop(ahead)
    sent = (sent, pump.turn(ahead))
    d_four = seg_rest(keep, after(come, sent), 2)
    d_four = exchange_seq(d_four.reshape(count, -1, 4, cols).transpose(0, 2, 1, 3).reshape(count, -1, cols), 0, 0)
    out, ahead, packed = mix(1, gr, (out, after(ahead, (sent, keep)), packed))
    while len(pump.done) < len(pump.values):
        token = pump.turn(ahead)
    cm_sums = [jnp.concatenate(pump.done[i : i + 2], axis=0) for i in (0, 2)] + pump.done[4:]
    cm_come = [lax.ppermute(value, "seg", near) for value in cm_sums]
    go1_cols = go1.finish(ahead).astype(HB)
    z = assembled(z_held, z_far, 1)
    d_out = mm_tn(z, go1_cols).astype(HB).reshape(segs, -1, cols)
    keep, come = seg_round(d_out, 1)
    d_out = (keep.astype(F) + come.astype(F)).astype(HB)
    keep, come = seg_round(d_out, 2)
    ahead, d_four, cm_sums = after((ahead, d_four, cm_sums), keep)
    out, _, _, packed = mix(2, gr, (out, ahead, packed))
    d_out = exchange_seq(seg_rest(keep, after(come, packed), 2).reshape(count, -1, cols), 0, 0)

    def joined(blocks, mats_in):
        return blocks.reshape(count, mats_in, -1, cols).transpose(1, 2, 0, 3).reshape(mats_in, -1, width).astype(F)

    d_mats = jnp.concatenate([joined(d_four, 4), joined(d_out, 1)], axis=0)
    cm_grads = tuple(
        jnp.where(bit == 0, jnp.concatenate([a, b], axis=0), jnp.concatenate([b, a], axis=0)).astype(F)
        for a, b in zip(cm_sums, after(cm_come, packed))
    )

    rest = scatter_seg(packed).T
    final = Scatter(lambda start: cut(out, start, rows, 0).astype(F), rows)
    final.hop()
    rest = exchange_seq(rest.reshape(count, -1, 2 * PAD), 0, 0).astype(F)
    input_grad = final.finish()
    rest = jnp.sum(rest, axis=0)
    rank_grad = jnp.stack([rest[:, :ranks], rest[:, PAD : PAD + ranks]])
    few = jnp.concatenate([rest[:, ranks:PAD], rest[:, PAD + ranks :]], axis=1).T
    vectors_grad = jnp.concatenate([few[0:3], few[32:37], few[17:18], few[16:17], few[18:20], few[8:12]], axis=0)
    return (block_out, input_grad, d_mats, rank_grad, vectors_grad, *cm_grads)


def solution(mesh):
    by_token = P(("seg", "seq"), None)
    in_specs = (
        by_token,
        P(None, ("seg", "seq"), None),
        P(None, ("seg", "seq"), None),
        P(),
        P("seg", None, None, None),
        P(None, "seq"),
        P("seq", None),
        P(None, "seq"),
        by_token,
    )
    out_specs = (
        by_token,
        by_token,
        P(None, ("seg", "seq"), None),
        P(None, ("seg", "seq"), None),
        P(None, ("seg", "seq")),
        P(None, "seq"),
        P("seq", None),
        P(None, "seq"),
    )
    return jax.shard_map(shards, mesh=mesh, in_specs=in_specs, out_specs=out_specs, check_vma=False)
```

```python
import functools
import jax
import jax.numpy as jnp
import numpy as np
from jax import lax
from jax.experimental import pallas as pl
from jax.experimental.pallas import tpu as pltpu
from jax.sharding import PartitionSpec as P

F = jnp.float32
HB = jnp.bfloat16
G = 64
B = 16
LANES = 128
MIX_RANK = 32
EPS_N = 1e-05
EPS_G = 0.00064
VMEM = 60 << 20
PAD = 256
FLOOR = -120.0


def mm(a, b):
    return jnp.dot(a, b, preferred_element_type=F)


def mm_nt(a, b):
    return lax.dot_general(a, b, (((1,), (1,)), ((), ())), preferred_element_type=F)


def mm_tn(a, b):
    return lax.dot_general(a, b, (((0,), (0,)), ((), ())), preferred_element_type=F)


def head_mask(dt):
    i = lax.broadcasted_iota(jnp.int32, (LANES, LANES), 0) // G
    j = lax.broadcasted_iota(jnp.int32, (LANES, LANES), 1) // G
    return (i == j).astype(dt)


def head_sum(x, ones):
    hi = x.astype(HB)
    lo = (x - hi.astype(F)).astype(HB)
    return mm(hi, ones) + mm(lo, ones)


def block_sums(d):
    row = lax.broadcasted_iota(jnp.int32, d.shape, 1)
    run = d
    for step in (1, 2, 4, 8):
        run = run + jnp.where(row >= step, pltpu.roll(run, step, 1), 0.0)
    return run


def pair_rows(s):
    if s < 7:
        return 0, 16
    return 8, 8


def pair_weight(excl, incl, s):
    first, rows = pair_rows(s)
    gap = excl[:, first : first + rows, :] - incl[:, s : s + 1, :]
    if s != 7:
        u = first + lax.broadcasted_iota(jnp.int32, gap.shape, 1)
        gap = jnp.where(u > s, gap, -1e30)
    return jnp.exp(gap)


def silu_parts(g):
    sig = 1.0 / (1.0 + jnp.exp(-g))
    return sig, g * sig


def fwd_body(groups, nb, r_ref, k_ref, v_ref, rate_ref, gp_ref, vec_ref, s0_ref,
             z_ref, y_ref, st_ref, state):
    @pl.when(pl.program_id(0) == 0)
    def _():
        state[...] = s0_ref[...]

    ones = head_mask(HB)
    keep = head_mask(F)
    rows = nb * B
    for g in range(groups):
        cols = slice(g * LANES, (g + 1) * LANES)

        def blocks(ref):
            return ref[:, cols].astype(F).reshape(nb, B, LANES)

        r, k, v = blocks(r_ref), blocks(k_ref), blocks(v_ref)
        decay = jnp.maximum(-jnp.exp(blocks(rate_ref)), FLOOR)
        bonus, gn_g, gn_b = (vec_ref[i : i + 1, cols] for i in range(3))
        incl = block_sums(decay)
        excl = incl - decay
        last = incl[:, B - 1 : B, :]
        rq = (r * jnp.exp(excl)).astype(HB)
        kk = (k * jnp.exp(last - incl)).astype(HB)
        whole = jnp.exp(last)
        vb = v.astype(HB)
        from_state = []
        st = state[g]
        for b in range(nb):
            stb = st.astype(HB)
            st_ref[b, g] = stb
            from_state.append(mm_nt(rq[b], stb))
            st = st * whole[b] + keep * mm_tn(vb[b], kk[b])
        state[g] = st
        bits = []
        for s in range(B - 1):
            first, n = pair_rows(s)
            e = pair_weight(excl, incl, s)
            bits.append((r[:, first : first + n, :] * k[:, s : s + 1, :] * e).astype(HB).reshape(nb * n, LANES))
        bits.append((r * k * bonus).astype(HB).reshape(rows, LANES))
        scores = mm(jnp.concatenate(bits, axis=0), ones)
        at = 0
        low = jnp.zeros((nb, 8, LANES), F)
        high = jnp.zeros((nb, 8, LANES), F)
        for s in range(B - 1):
            first, n = pair_rows(s)
            part = scores[at : at + nb * n].reshape(nb, n, LANES) * v[:, s : s + 1, :]
            at += nb * n
            if n == 16:
                low = low + part[:, :8]
                high = high + part[:, 8:]
            else:
                high = high + part
        own = scores[at : at + rows].reshape(nb, B, LANES) * v
        y = jnp.concatenate([low, high], axis=1) + own
        y = y.reshape(rows, LANES) + jnp.concatenate(from_state, axis=0)
        y_ref[:, cols] = y
        center = y - head_sum(y, ones) * (1.0 / G)
        spread = head_sum(center * center, ones) * (1.0 / G)
        normed = center * lax.rsqrt(spread + EPS_G)
        _, act = silu_parts(gp_ref[:, cols])
        z_ref[:, cols] = ((normed * gn_g + gn_b) * act).astype(HB)


def wkv_forward(r, k, v, rate, gp, vec, start, step_tokens=128):
    tokens, width = r.shape
    groups = width // LANES
    nb = step_tokens // B
    steps = tokens // step_tokens
    row = pl.BlockSpec((step_tokens, width), lambda i: (i, 0))
    full = lambda shape: pl.BlockSpec(shape, lambda i: (0,) * len(shape))
    return pl.pallas_call(
        functools.partial(fwd_body, groups, nb),
        grid=(steps,),
        in_specs=[row, row, row, row, row, full(vec.shape), full(start.shape)],
        out_specs=[row, row, pl.BlockSpec((nb, groups, LANES, LANES), lambda i: (i, 0, 0, 0))],
        out_shape=[
            jax.ShapeDtypeStruct((tokens, width), HB),
            jax.ShapeDtypeStruct((tokens, width), F),
            jax.ShapeDtypeStruct((tokens // B, groups, LANES, LANES), HB),
        ],
        scratch_shapes=[pltpu.VMEM((groups, LANES, LANES), F)],
        cost_estimate=pl.CostEstimate(flops=tokens * width * 95000, transcendentals=tokens * width * 16, bytes_accessed=tokens * width * 40),
        name="wkv_forward",
    )(r, k, v, rate, gp, vec, start)


def bwd_body(groups, nb, r_ref, k_ref, v_ref, rate_ref, gp_ref, y_ref, gz_ref, vec_ref, st_ref, adj_in, sums_in, *rest):
    gr_ref, gk_ref, gv_ref, gg_ref, gd_ref, adj, sums_ref = rest[-7:]

    @pl.when(pl.program_id(0) == 0)
    def _():
        adj[...] = adj_in[...]
        sums_ref[...] = sums_in[...]

    ones = head_mask(HB)
    keep = head_mask(F)
    rows = nb * B
    cols_of = []
    for s in range(B - 1):
        first, n = pair_rows(s)
        cols_of.append((s, first, n))
    for g in range(groups):
        cols = slice(g * LANES, (g + 1) * LANES)

        def blocks(x):
            return x.astype(F).reshape(nb, B, LANES)

        r, k, v = blocks(r_ref[:, cols]), blocks(k_ref[:, cols]), blocks(v_ref[:, cols])
        raw = -jnp.exp(blocks(rate_ref[:, cols]))
        decay = jnp.maximum(raw, FLOOR)
        bonus, gn_g, gn_b = (vec_ref[i : i + 1, cols] for i in range(3))
        y, gp, gz = y_ref[:, cols], gp_ref[:, cols], gz_ref[:, cols]
        center = y - head_sum(y, ones) * (1.0 / G)
        spread = head_sum(center * center, ones) * (1.0 / G)
        inv = lax.rsqrt(spread + EPS_G)
        normed = center * inv
        sig, act = silu_parts(gp)
        gated = gz * act
        gg_ref[:, cols] = (gz * (normed * gn_g + gn_b) * sig * (1.0 + gp * (1.0 - sig))).astype(HB)
        sums_ref[2:3, cols] += jnp.sum(gated * normed, axis=0, keepdims=True)
        sums_ref[3:4, cols] += jnp.sum(gated, axis=0, keepdims=True)
        gn = gated * gn_g
        gy = inv * (gn - head_sum(gn, ones) * (1.0 / G) - normed * (head_sum(gn * normed, ones) * (1.0 / G)))
        gy = gy.reshape(nb, B, LANES)
        incl = block_sums(decay)
        excl = incl - decay
        last = incl[:, B - 1 : B, :]
        to_start = jnp.exp(excl)
        to_end = jnp.exp(last - incl)
        whole = jnp.exp(last)
        rq = (r * to_start).astype(HB)
        kk = (k * to_end).astype(HB)
        vb = v.astype(HB)
        gyb = gy.astype(HB)
        lt = adj[g]
        gr_state, gk_state, gv_state, crossing = [None] * nb, [None] * nb, [None] * nb, [None] * nb
        for b in reversed(range(nb)):
            ltb = lt.astype(HB)
            stb = st_ref[b, g]
            gr_state[b] = mm(gyb[b], stb)
            gk_state[b] = mm(vb[b], ltb)
            gv_state[b] = mm_nt(kk[b], ltb)
            crossing[b] = jnp.sum(lt * stb.astype(F), axis=0, keepdims=True) * whole[b]
            lt = lt * whole[b] + keep * mm_tn(gyb[b], rq[b])
        adj[g] = lt
        stack = lambda parts: jnp.concatenate(parts, axis=0).reshape(nb, B, LANES)
        gr_in = stack(gr_state) * to_start
        gk_out = stack(gk_state) * to_end
        gv = stack(gv_state)
        e_bits, m_bits, a_bits, w_cache = [], [], [], []
        for s, first, n in cols_of:
            e = pair_weight(excl, incl, s)
            w_cache.append(e)
            a_bits.append((r[:, first : first + n] * k[:, s : s + 1] * e).astype(HB).reshape(nb * n, LANES))
            m_bits.append((gy[:, first : first + n] * v[:, s : s + 1]).astype(HB).reshape(nb * n, LANES))
        a_bits.append((r * k * bonus).astype(HB).reshape(rows, LANES))
        m_bits.append((gy * v).astype(HB).reshape(rows, LANES))
        scores = mm(jnp.concatenate(a_bits, axis=0), ones)
        dots = mm(jnp.concatenate(m_bits, axis=0), ones)
        at = 0
        low = jnp.zeros((nb, 8, LANES), F)
        high = jnp.zeros((nb, 8, LANES), F)
        p1, p2, p3 = [], [], []
        for (s, first, n), e in zip(cols_of, w_cache):
            m = dots[at : at + nb * n].reshape(nb, n, LANES)
            a = scores[at : at + nb * n].reshape(nb, n, LANES)
            at += nb * n
            me = m * e
            part = me * k[:, s : s + 1]
            if n == 16:
                low = low + part[:, :8]
                high = high + part[:, 8:]
            else:
                high = high + part
            mer = me * r[:, first : first + n]
            p1.append(mer)
            p2.append(a * gy[:, first : first + n])
            p3.append(mer * k[:, s : s + 1])
        a_own = scores[at : at + rows].reshape(nb, B, LANES)
        m_own = dots[at : at + rows].reshape(nb, B, LANES)
        gr = gr_in + jnp.concatenate([low, high], axis=1) + m_own * bonus * k
        gr_ref[:, cols] = gr.reshape(rows, LANES).astype(HB)
        p3.append(gr_in * r)
        p3.append(gk_out * k)
        total = sum(n for _, _, n in cols_of)
        col_s = jnp.concatenate([jnp.full((B, n), s, jnp.int32) for s, _, n in cols_of], axis=1)
        t = lax.broadcasted_iota(jnp.int32, (B, total), 0)
        pick = (col_s == t).astype(HB)
        col_u = jnp.concatenate([first + lax.broadcasted_iota(jnp.int32, (B, n), 1) for _, first, n in cols_of], axis=1)
        around = ((col_s < t) & (col_u > t)).astype(HB)
        i = lax.broadcasted_iota(jnp.int32, (B, B), 0)
        j = lax.broadcasted_iota(jnp.int32, (B, B), 1)
        around = jnp.concatenate([around, (j > i).astype(HB), (j < i).astype(HB)], axis=1)
        gk_pairs, gv_pairs, gd = [], [], []
        for b in range(nb):
            gk_pairs.append(mm(pick, jnp.concatenate([p[b] for p in p1], axis=0).astype(HB)))
            gv_pairs.append(mm(pick, jnp.concatenate([p[b] for p in p2], axis=0).astype(HB)))
            gd.append(mm(around, jnp.concatenate([p[b] for p in p3], axis=0).astype(HB)) + crossing[b])
        gk = gk_out + stack(gk_pairs) + m_own * bonus * r
        gk_ref[:, cols] = gk.reshape(rows, LANES).astype(HB)
        gv = gv + stack(gv_pairs) + a_own * gy
        gv_ref[:, cols] = gv.reshape(rows, LANES).astype(HB)
        grate = (stack(gd) * raw).reshape(rows, LANES)
        gd_ref[:, cols] = grate.astype(HB)
        sums_ref[0:1, cols] += jnp.sum((m_own * r * k).reshape(rows, LANES), axis=0, keepdims=True)
        sums_ref[1:2, cols] += jnp.sum(grate, axis=0, keepdims=True)


def wkv_backward(r, k, v, rate, gp, y, gz, vec, states, at, count, adj, sums, outs, step_tokens=128):
    tokens, width = r.shape
    groups = width // LANES
    nb = step_tokens // B
    steps = count // step_tokens
    full = lambda shape: pl.BlockSpec(shape, lambda i: (0,) * len(shape))
    low = jax.ShapeDtypeStruct((tokens, width), HB)
    top = at // step_tokens + steps - 1
    high = gz.shape[0] // step_tokens - 1 - (tokens - at - count) % gz.shape[0] // step_tokens
    row = pl.BlockSpec((step_tokens, width), lambda i: (top - i, 0))
    state = pl.BlockSpec((nb, groups, LANES, LANES), lambda i: (top - i, 0, 0, 0))
    *outs, adj, sums = pl.pallas_call(
        functools.partial(bwd_body, groups, nb),
        grid=(steps,),
        in_specs=[row] * 6 + [pl.BlockSpec((step_tokens, width), lambda i: (high - i, 0))]
        + [full(vec.shape), state, full(adj.shape), full(sums.shape)] + [pl.BlockSpec(memory_space=pl.ANY)] * len(outs),
        out_specs=[row] * 5 + [full(adj.shape), full(sums.shape)],
        out_shape=[low] * 5 + [jax.ShapeDtypeStruct(adj.shape, F), jax.ShapeDtypeStruct(sums.shape, F)],
        input_output_aliases={11 + i: i for i in range(len(outs))},
        cost_estimate=pl.CostEstimate(flops=count * width * 184000, transcendentals=count * width * 20, bytes_accessed=count * width * 60),
        name="wkv_backward",
    )(r, k, v, rate, gp, y, gz, vec, states, adj, sums, *outs)
    return outs, adj, sums


def normalize(values):
    center = values - jnp.mean(values, axis=-1, keepdims=True)
    inverse = lax.rsqrt(jnp.mean(center * center, axis=-1, keepdims=True) + EPS_N)
    return center * inverse, inverse


def normalize_back(grad, normed, inverse, gain):
    scaled = grad * gain
    return inverse * (
        scaled
        - jnp.mean(scaled, axis=-1, keepdims=True)
        - normed * jnp.mean(scaled * normed, axis=-1, keepdims=True)
    )


def shift_down(values, first_row):
    row = lax.broadcasted_iota(jnp.int32, values.shape, 0)
    return jnp.where(row == 0, first_row, pltpu.roll(values, 1, 0))


def shift_up(values, last_row):
    row = lax.broadcasted_iota(jnp.int32, values.shape, 0)
    count = values.shape[0]
    return jnp.where(row == count - 1, last_row, pltpu.roll(values, count - 1, 0))


def whole(array):
    return pl.BlockSpec(array.shape, lambda i: (0,) * array.ndim, pipeline_mode=pl.Buffered(1))


def lane_groups(shape):
    return lax.broadcasted_iota(jnp.int32, shape, 1) // MIX_RANK


def weight_cols(refs, slot):
    for ref in refs:
        yield ref[:, slot].reshape(ref.shape[0] * ref.shape[2], ref.shape[3])


def mix_forward_body(segs, x_ref, prm_ref, down_ref, up_ref, at_ref, *rest):
    w_refs = rest[:segs]
    r_ref, k_ref, v_ref, gp_ref, rate_ref, t_ref, xr_ref, xk_ref, xv_ref, xg_ref, last = rest[segs:]

    @pl.when(pl.program_id(0) == 0)
    def _():
        last[...] = jnp.zeros_like(last)

    prm = lambda i: prm_ref[i : i + 1, :]
    width, cols = x_ref.shape[1], r_ref.shape[1]
    normed, _ = normalize(x_ref[...].astype(F))
    xn = normed * prm(0) + prm(1)
    dx = shift_down(xn, last[0:1, :]) - xn
    last[0:1, :] = xn[xn.shape[0] - 1 :, :]
    t_mix = jnp.tanh(mm((xn + dx * prm(2)).astype(HB), down_ref[...]))
    group = lane_groups(t_mix.shape)
    low = t_mix.astype(HB)

    def mixed(j):
        own = jnp.where(group == j, low, jnp.zeros_like(low))
        return (xn + dx * (prm(3 + j) + mm_nt(own, up_ref[...]))).astype(HB)

    t_dec = jnp.tanh(mm(mixed(0), down_ref[...]))
    t_ref[...] = jnp.where(group < 5, t_mix, t_dec)
    dec = t_dec.astype(HB)
    own_cols = pl.ds(pl.multiple_of(at_ref[0], cols), cols)
    rate_ref[...] = prm_ref[8:9, own_cols] + mm_nt(jnp.where(group < 5, jnp.zeros_like(dec), dec), up_ref[own_cols, :])
    part = width // segs
    for j, slot, x_out, y_out in ((1, 1, xk_ref, k_ref), (2, 2, xv_ref, v_ref), (3, 0, xr_ref, r_ref), (4, 3, xg_ref, gp_ref)):
        x_out[...] = mixed(j)
        total = None
        for i, w in enumerate(weight_cols(w_refs, slot)):
            term = mm(x_out[:, pl.ds(pl.multiple_of(at_ref[1 + i], part), part)], w)
            total = term if total is None else total + term
        y_out[...] = total.astype(y_out.dtype)


def rank_halves(width):
    half = lambda h: pl.BlockSpec((width, PAD), lambda i, h=h: (0, h), pipeline_mode=pl.Buffered(1))
    return [half(0), half(1)]


SCALARS = pl.BlockSpec(memory_space=pltpu.SMEM)


def mix_forward(x, prm, rank, at, mats, tile=256):
    total, width = x.shape
    cols = mats[0].shape[3]
    row = lambda n: pl.BlockSpec((tile, n), lambda i: (i, 0))
    shape = lambda n, dt: jax.ShapeDtypeStruct((total, n), dt)
    return pl.pallas_call(
        functools.partial(mix_forward_body, len(mats)),
        grid=(total // tile,),
        in_specs=[row(width), whole(prm)] + rank_halves(width) + [SCALARS] + [whole(a) for a in mats],
        out_specs=[row(cols)] * 5 + [row(PAD)] + [row(width)] * 4,
        out_shape=[shape(cols, HB)] * 3 + [shape(cols, F)] * 2 + [shape(PAD, F)] + [shape(width, HB)] * 4,
        scratch_shapes=[pltpu.VMEM((8, width), F)],
        compiler_params=pltpu.CompilerParams(vmem_limit_bytes=VMEM),
        cost_estimate=pl.CostEstimate(flops=total * width * 13700, transcendentals=total * 512, bytes_accessed=total * width * 12),
        name="mix_forward",
    )(x, prm, rank, rank, at, *mats)


def residual_forward_body(pieces, x_ref, w_ref, prm_ref, recept_ref, go_ref, at_ref, *rest):
    z_refs = rest[: pieces + 1]
    x1_ref, ck_ref, cr_ref, sg_ref, gkv_ref, last = rest[pieces + 1 :]

    @pl.when(pl.program_id(0) == 0)
    def _():
        last[...] = jnp.zeros_like(last)

    prm = lambda i: prm_ref[i : i + 1, :]
    cols = recept_ref.shape[1]
    x1 = x_ref[...].astype(F)
    far = jnp.where(pl.program_id(0) < pl.num_programs(0) // 2, z_refs[pieces - 1][...], z_refs[pieces][...])
    for i, z in enumerate([ref[...] for ref in z_refs[: pieces - 1]] + [far]):
        x1 = x1 + mm(z, w_ref[pl.ds(pl.multiple_of(at_ref[i], cols), cols), :])
    x1_ref[...] = x1
    normed, _ = normalize(x1)
    xs = (normed * prm(12) + prm(13)).astype(HB).astype(F)
    dxs = shift_down(xs, last[0:1, :]) - xs
    last[0:1, :] = xs[xs.shape[0] - 1 :, :]
    ck_ref[...] = (xs + dxs * prm(14)).astype(HB)
    cr = (xs + dxs * prm(15)).astype(HB)
    cr_ref[...] = cr
    sg = 1.0 / (1.0 + jnp.exp(-mm(cr, recept_ref[...])))
    sg_ref[...] = sg
    gkv_ref[...] = (go_ref[...].astype(F) * sg).astype(HB)


def residual_forward(x, z, z_far, at, w_output, prm, recept, go_cols, tile=256):
    total, width = x.shape
    cols = recept.shape[1]
    half = total // tile // 2
    row = lambda n: pl.BlockSpec((tile, n), lambda i: (i, 0))
    shape = lambda n, dt: jax.ShapeDtypeStruct((total, n), dt)
    halves = [pl.BlockSpec((tile, cols), lambda i: (jnp.minimum(i, half - 1), 0)), pl.BlockSpec((tile, cols), lambda i: (jnp.maximum(i - half, 0), 0))]
    return pl.pallas_call(
        functools.partial(residual_forward_body, len(z) + 1),
        grid=(total // tile,),
        in_specs=[row(width), whole(w_output), whole(prm), whole(recept), row(cols), SCALARS] + [row(cols)] * len(z) + halves,
        out_specs=[row(width)] * 3 + [row(cols)] * 2,
        out_shape=[shape(width, F), shape(width, HB), shape(width, HB), shape(cols, F), shape(cols, HB)],
        scratch_shapes=[pltpu.VMEM((8, width), F)],
        compiler_params=pltpu.CompilerParams(vmem_limit_bytes=VMEM),
        cost_estimate=pl.CostEstimate(flops=total * width * 12000, transcendentals=total * cols, bytes_accessed=total * width * 12),
        name="residual_forward",
    )(x, w_output, prm, recept, go_cols, at, *z, *z_far)


def residual_backward_body(closes, x1_ref, before_ref, go_ref, ghp_ref, gsp_ref, key_ref, recept_ref, w_ref, prm_ref,
                           sums_in, ahead_in, *rest):
    gx1_ref, gz_ref, sums_ref, ahead = rest[-4:]
    at = pl.program_id(0)

    @pl.when(at == 0)
    def _():
        ahead[...] = ahead_in[...]
        sums_ref[...] = sums_in[...]

    prm = lambda i: prm_ref[i : i + 1, :]
    normed, inverse = normalize(x1_ref[...])
    xs = (normed * prm(12) + prm(13)).astype(HB).astype(F)
    other, _ = normalize(before_ref[...])
    other = (other[7:8, :] * prm(12) + prm(13)).astype(HB).astype(F)
    if closes:
        other = jnp.where(at == pl.num_programs(0) - 1, 0.0, other)
    dxs = shift_down(xs, other) - xs
    gck = mm_nt(ghp_ref[...], key_ref[...])
    gcr = mm_nt(gsp_ref[...], recept_ref[...])
    moved = gck * prm(14) + gcr * prm(15)
    gxs = gck + gcr - moved + shift_up(moved, ahead[0:1, :])
    ahead[0:1, :] = moved[0:1, :]
    total = lambda a: jnp.sum(a, axis=0, keepdims=True)
    sums_ref[0:1, :] += total(gxs * normed)
    sums_ref[1:2, :] += total(gxs)
    sums_ref[2:3, :] += total(gck * dxs)
    sums_ref[3:4, :] += total(gcr * dxs)
    gx1 = (go_ref[...].astype(F) + normalize_back(gxs, normed, inverse, prm(12))).astype(HB)
    gx1_ref[...] = gx1
    gz_ref[...] = mm_nt(gx1, w_ref[...]).astype(HB)


def residual_backward(x1, go_own, ghp, gsp, key, recept, w_output, prm, part, parts, sums, ahead, tile=256):
    total, width = x1.shape
    steps = total // tile // parts
    top = total // tile - 1 - part * steps
    row = lambda n: pl.BlockSpec((tile, n), lambda i: (top - i, 0))
    to = lambda n: pl.BlockSpec((tile, n), lambda i: (steps - 1 - i, 0))
    before = pl.BlockSpec((8, width), lambda i: (jnp.maximum((top - i) * (tile // 8) - 1, 0), 0))
    low = jax.ShapeDtypeStruct((total // parts, width), HB)
    few = jax.ShapeDtypeStruct((8, width), F)
    const = pl.BlockSpec((8, width), lambda i: (0, 0))
    flops = steps * tile * width * 17500
    return pl.pallas_call(
        functools.partial(residual_backward_body, part == parts - 1),
        grid=(steps,),
        in_specs=[row(width), before, row(width), row(ghp.shape[1]), row(gsp.shape[1])] + [whole(a) for a in (key, recept, w_output, prm)] + [const, const],
        out_specs=[to(width), to(width), const, const],
        out_shape=[low, low, few, few],
        compiler_params=pltpu.CompilerParams(vmem_limit_bytes=VMEM),
        cost_estimate=pl.CostEstimate(flops=flops, transcendentals=total, bytes_accessed=steps * tile * width * 12),
        name="residual_backward",
    )(x1, x1, go_own, ghp, gsp, key, recept, w_output, prm, sums, ahead)


def mix_backward_body(opens, closes, x_ref, before_ref, gr_ref, gk_ref, gv_ref, gg_ref, grb_ref, t_ref, gx1_ref,
                      prm_ref, two_ref, heads_ref, up_ref, downt_ref, upt_ref, at_ref, w_ref, *rest):
    given = rest[: 0 if opens else 3]
    out_ref, ahead, packed, *more = rest[len(given) :]
    gmix, mstack = more[-2:]
    at = pl.program_id(0)
    width, cols = x_ref.shape[1], gr_ref.shape[1]
    tile = x_ref.shape[0]

    @pl.when(at == 0)
    def _():
        if opens:
            ahead[...] = jnp.zeros_like(ahead)
            packed[...] = jnp.zeros_like(packed)
        else:
            ahead[...] = given[1][...]
            packed[...] = given[2][...]

    own_cols = pl.ds(pl.multiple_of(at_ref[0], cols), cols)
    prm = lambda i: prm_ref[i : i + 1, :]
    normed, inverse = normalize(x_ref[...].astype(F))
    xn = normed * prm(0) + prm(1)
    other, _ = normalize(before_ref[...].astype(F))
    other = other[15:16, :] * prm(0) + prm(1)
    if closes:
        first_tile = at == pl.num_programs(0) - 1
        other = jnp.where(first_tile, 0.0, other)
    dx = shift_down(xn, other) - xn
    t = t_ref[...]
    slope = 1.0 - t * t
    low = t.astype(HB)
    group = lane_groups(t.shape)
    lane = lax.broadcasted_iota(jnp.int32, t.shape, 1)
    zero = jnp.zeros_like(low)
    dec = jnp.where((group < 5) | (group == 7), zero, low)
    ge = jnp.where(group < 5, 0.0, mm(grb_ref[...], up_ref[own_cols, :]) * slope).astype(HB)
    packed[PAD : 2 * PAD, own_cols] += mm_tn(dec, grb_ref[...])
    gdx = gsum = gm = None
    for j, (slot, g_ref) in enumerate(((None, None), (1, gk_ref), (2, gv_ref), (0, gr_ref), (3, gg_ref))):
        own = jnp.where(group == j, low, zero)
        mstack[j * tile : (j + 1) * tile, :] = jnp.where(lane == 7 * MIX_RANK + j, jnp.ones_like(own), own)
        lerp = prm(3 + j) + mm(own, upt_ref[...])
        if j == 0:
            gx = mm(ge, downt_ref[...])
            x_w = (xn + dx * lerp).astype(HB)
        else:
            gx = mm_nt(g_ref[...], w_ref[:, slot].reshape(width, cols))
        moved = gx * lerp
        gdx = moved if gdx is None else gdx + moved
        gsum = gx if gsum is None else gsum + gx
        bits = (gx * dx).astype(HB)
        gmix[j * tile : (j + 1) * tile, :] = bits
        part_m = jnp.where(group == j, mm(bits, up_ref[...]), 0.0)
        gm = part_m if gm is None else gm + part_m
    gm = (gm * slope).astype(HB)
    gxm = mm(gm, downt_ref[...])
    gdx = gdx + gxm * prm(2)
    gxn = gsum + gxm - gdx + shift_up(gdx, ahead[0:1, :])
    ahead[0:1, :] = gdx[0:1, :]
    total = lambda a: jnp.sum(a, axis=0, keepdims=True)
    xm = (xn + dx * prm(2)).astype(HB)
    packed[:PAD, :] += mm_tn(jnp.concatenate([gm, ge], axis=0), jnp.concatenate([xm, x_w], axis=0))
    packed[PAD : 2 * PAD, :] += mm_tn(mstack[...], gmix[...])
    spare = 7 * MIX_RANK
    packed[spare : spare + 1, :] += total(gxn * normed)
    packed[spare + 1 : spare + 2, :] += total(gxn)
    packed[spare + 2 : spare + 3, :] += total(gxm * dx)
    out_ref[...] = (gx1_ref[...].astype(F) + normalize_back(gxn, normed, inverse, prm(0))).astype(HB)
    if closes:
        @pl.when(first_tile)
        def _():
            packed[spare + 8 : spare + 16, :] += two_ref[...]
            packed[spare + 16 : spare + 24, own_cols] += heads_ref[...]
            block = more[0].shape[2]
            for i in range(more[0].shape[0]):
                more[0][i] = packed[:, i * block : (i + 1) * block].astype(HB)


def mix_backward(x, grads, t, gx1, mats, rank, down_t, up_t, prm, two, heads, at, segs, first_tile, steps, given, tile=256):
    total, width = x.shape
    cols = mats.shape[3]
    lines = 2 * PAD
    shape = jax.ShapeDtypeStruct
    fixed = lambda *s: pl.BlockSpec(s, lambda i: (0,) * len(s))
    top = first_tile
    row = lambda n: pl.BlockSpec((tile, n), lambda i: (top - i, 0))
    before = pl.BlockSpec((16, width), lambda i: (jnp.maximum((top - i) * (tile // 16) - 1, 0), 0))
    closes = top - steps < 0
    return pl.pallas_call(
        functools.partial(mix_backward_body, not given, closes),
        grid=(steps,),
        in_specs=[row(width), before] + [row(cols)] * 5 + [row(PAD), row(width)]
        + [whole(a) for a in (prm, two, heads)] + rank_halves(width)[1:] + [whole(down_t), whole(up_t), SCALARS, whole(mats)]
        + ([pl.BlockSpec(memory_space=pl.ANY), whole(given[1]), whole(given[2])] if given else []),
        out_specs=[row(width), fixed(8, width), fixed(lines, width)] + [fixed(segs, lines, width // segs)] * closes,
        out_shape=[shape((total, width), HB), shape((8, width), F), shape((lines, width), F)] + [shape((segs, lines, width // segs), HB)] * closes,
        input_output_aliases={17: 0} if given else {},
        scratch_shapes=[pltpu.VMEM((5 * tile, width), HB), pltpu.VMEM((5 * tile, PAD), HB)],
        compiler_params=pltpu.CompilerParams(vmem_limit_bytes=VMEM),
        cost_estimate=pl.CostEstimate(flops=steps * tile * width * 35000, transcendentals=total, bytes_accessed=steps * tile * width * 10),
        name="mix_backward",
    )(x, x, *grads, t, gx1, prm, two, heads, rank, down_t, up_t, at, mats, *given)


def outer_parts_body(at_ref, grad_ref, *rest):
    *parts, low_ref, high_ref, out_ref = rest
    cols = grad_ref.shape[1]
    half = low_ref.shape[0]
    rows = lambda i: pl.ds(pl.multiple_of(at_ref[i], cols), cols)
    for i, ref in enumerate(parts):
        out_ref[rows(i), :] = mm_tn(ref[...], grad_ref[...]).astype(HB)
    far = mm_tn(low_ref[...], grad_ref[:half, :]) + mm_tn(high_ref[...], grad_ref[half:, :])
    out_ref[rows(len(parts)), :] = far.astype(HB)


def outer_parts(parts, far, at, grad, width):
    total, cols = grad.shape
    everything = lambda a: pl.BlockSpec(a.shape, lambda: (0,) * a.ndim)
    return pl.pallas_call(
        outer_parts_body,
        in_specs=[SCALARS] + [everything(a) for a in (grad, *parts, *far)],
        out_specs=pl.BlockSpec((width, cols), lambda: (0, 0)),
        out_shape=jax.ShapeDtypeStruct((width, cols), HB),
        compiler_params=pltpu.CompilerParams(vmem_limit_bytes=VMEM),
        cost_estimate=pl.CostEstimate(flops=2 * total * cols * width, transcendentals=0, bytes_accessed=2 * total * width),
        name="outer_parts",
    )(at, grad, *parts, *far)


def join_body(bit_ref, mine_ref, other_ref, out_ref):
    out_ref[...] = jnp.where(pl.program_id(0) == bit_ref[0], mine_ref[...], other_ref[...]).astype(F)


def join_halves(mine, other, bit):
    count, width = mine.shape
    rows = count // 4 if count % 64 == 0 else count
    steps = count // rows
    held = lambda own: pl.BlockSpec((rows, width), lambda h, i, b: (jnp.where((h == b[0]) == own, i, 0), 0))
    return pl.pallas_call(
        join_body,
        grid_spec=pltpu.PrefetchScalarGridSpec(
            num_scalar_prefetch=1,
            grid=(2, steps),
            in_specs=[held(True), held(False)],
            out_specs=pl.BlockSpec((rows, width), lambda h, i, b: (h * steps + i, 0)),
        ),
        out_shape=jax.ShapeDtypeStruct((2 * count, width), F),
        cost_estimate=pl.CostEstimate(flops=0, transcendentals=0, bytes_accessed=12 * count * width),
        name="join_halves",
    )(bit, mine, other)


def ring_of(count):
    deep = 4 if count % 4 == 0 and count >= 8 else 1
    wide = count // deep
    if deep == 1 or wide == 1:
        return list(range(count))
    path = []
    for z in range(deep):
        xs = range(1, wide) if z % 2 == 0 else range(wide - 1, 0, -1)
        path += [z * wide + x for x in xs]
    return path + [z * wide for z in reversed(range(deep))]


class Ring:
    def __init__(self, scale=1):
        self.count = lax.axis_size("seq")
        self.path = ring_of(self.count)
        place = [self.path.index(i) for i in range(self.count)]
        table = [[self.path[(place[i] + away) % self.count] for away in range(self.count)] for i in range(self.count)]
        self.scale = np.uint32(scale)
        here = lax.axis_index("seq").astype(jnp.uint32)
        self.row = lax.dynamic_slice(np.array(table, np.uint32), (here, np.uint32(0)), (1, self.count))
        self.right = [(self.path[i], self.path[(i + 1) % self.count]) for i in range(self.count)]
        self.left = [(b, a) for a, b in self.right]

    def owner(self, away):
        away %= self.count
        index = lax.reshape(lax.slice(self.row, (0, away), (1, away + 1)), ())
        return index * self.scale if self.scale > 1 else index


def starts(ndim, at):
    return [at.get(d, np.uint32(0)) for d in range(ndim)]


def cut(array, start, size, dim):
    sizes = list(array.shape)
    sizes[dim] = size
    return lax.dynamic_slice(array, starts(array.ndim, {dim: start}), sizes)


def put(array, piece, at):
    return lax.dynamic_update_slice(array, piece, starts(array.ndim, at))


def ring_hops(part, others=()):
    ring = Ring()
    half = part.shape[0] // 2
    held = [(0, part)]
    going_right = going_left = part
    for step in range(1, ring.count // 2):
        going_right = lax.ppermute(going_right, "seq", ring.right)
        going_left = lax.ppermute(going_left, "seq", ring.left)
        if step <= len(others):
            going_right, going_left = after((going_right, going_left), others[step - 1])
        held += [(-step, going_right), (step, going_left)]
    far = lax.ppermute(going_right[:half], "seq", ring.right), lax.ppermute(going_left[half:], "seq", ring.left)
    return held, far


def assembled(held, far, dim):
    part = held[0][1]
    size = part.shape[dim]
    ring = Ring(size)
    shape = list(part.shape)
    shape[dim] = size * ring.count
    out = jnp.zeros(shape, part.dtype)
    for away, piece in held:
        out = put(out, piece, {dim: ring.owner(away)})
    half = part.shape[0] // 2
    start = ring.owner(ring.count // 2)
    out = put(out, far[0], {dim: start})
    low = {dim: start + np.uint32(half)} if dim == 0 else {dim: start, 0: np.uint32(half)}
    return put(out, far[1], low)


def gather_seq(part, dim, others=()):
    return assembled(*ring_hops(part, others), dim)


def after(value, other):
    return lax.optimization_barrier((value, other))[0]


class Scatter:
    def __init__(self, piece_of, scale):
        self.ring = Ring(scale)
        self.right, self.left = self.ring.right, self.ring.left
        self.piece_of = piece_of
        self.hops = self.step = self.ring.count // 2
        self.going = None

    def term(self, away):
        return self.piece_of(self.ring.owner(away))

    def hop(self, other=None):
        if self.going is None:
            last = self.term(self.hops)
            half = last.shape[0] // 2
            more, less = last[:half], last[half:]
        else:
            from_left, from_right = self.going if other is None else after(self.going, other)
            more, less = self.term(self.step), self.term(-self.step)
            if self.step == self.hops - 1:
                half = from_left.shape[0]
                more = jnp.concatenate([more[:half] + from_left.astype(F), more[half:]], axis=0)
                less = jnp.concatenate([less[:half], less[half:] + from_right.astype(F)], axis=0)
            else:
                more = more + from_left.astype(F)
                less = less + from_right.astype(F)
        sent = more.astype(HB), less.astype(HB)
        self.going = lax.ppermute(sent[0], "seq", self.right), lax.ppermute(sent[1], "seq", self.left)
        self.step -= 1
        return sent

    def finish(self, other=None):
        while self.step > 0:
            self.hop()
        from_left, from_right = self.going if other is None else after(self.going, other)
        return self.term(0) + from_left.astype(F) + from_right.astype(F)


def scatter_seq(piece_of, scale):
    return Scatter(piece_of, scale).finish()


def gather_seg(part):
    count = lax.axis_size("seg")
    held = {0: part}
    step = count // 2
    while step:
        pairs = [(i, i ^ step) for i in range(count)]
        held.update({i ^ step: lax.ppermute(value, "seg", pairs) for i, value in list(held.items())})
        step //= 2
    return [held[i] for i in range(count)]


def seg_bit(step):
    return (lax.axis_index("seg").astype(jnp.uint32) & np.uint32(step)) // np.uint32(step) if step > 1 else lax.axis_index("seg").astype(jnp.uint32) & np.uint32(1)


def seg_round(parts, step, dim=0):
    count = lax.axis_size("seg")
    bit = seg_bit(step)
    shape = list(parts.shape)
    shaped = parts.reshape(shape[:dim] + [shape[dim] // 2, 2] + shape[dim + 1 :])
    keep = lax.squeeze(cut(shaped, bit, 1, dim + 1), (dim + 1,))
    give = lax.squeeze(cut(shaped, np.uint32(1) - bit, 1, dim + 1), (dim + 1,))
    return keep, lax.ppermute(give, "seg", [(i, i ^ step) for i in range(count)])


def seg_rest(keep, come, step, dim=0):
    parts = (keep.astype(F) + come.astype(F)).astype(HB)
    while step * 2 < lax.axis_size("seg"):
        step *= 2
        keep, come = seg_round(parts, step, dim)
        parts = (keep.astype(F) + come.astype(F)).astype(HB)
    return lax.squeeze(parts, (dim,))


def scatter_seg(parts):
    return seg_rest(*seg_round(parts, 1), 1)


class Pump:
    def __init__(self, values):
        count = lax.axis_size("seg")
        self.values, self.done, self.coming = list(values), [], None
        self.rounds = [[(i, i ^ (2 << n)) for i in range(count)] for n in range((count // 2).bit_length() - 1)]

    def send(self):
        self.coming = [lax.ppermute(value, "seg", self.rounds[0]) for value in self.values[len(self.done)]]

    def turn(self, other):
        at = len(self.done)
        if at == len(self.values):
            return other
        if self.coming is None:
            self.values[at] = after(self.values[at], other)
            self.send()
            return self.values[at]
        come = after(self.coming, other)
        sums = [(a.astype(F) + b.astype(F)).astype(HB) for a, b in zip(self.values[at], come)]
        for pairs in self.rounds[1:]:
            sums = [(a.astype(F) + lax.ppermute(a, "seg", pairs).astype(F)).astype(HB) for a in sums]
        self.done.append(sums)
        if at + 1 < len(self.values):
            self.values[at + 1] = after(self.values[at + 1], sums)
            self.send()
        return sums


def exchange_seq(value, split, join):
    return lax.all_to_all(value, "seq", split_axis=split, concat_axis=join, tiled=True)


def shards(tokens, tm_mats, low_rank, params, opening, cm_key, cm_value, cm_recept, out_grad):
    rows, width = tokens.shape
    count = lax.axis_size("seq")
    segs = lax.axis_size("seg")
    here = lax.axis_index("seq").astype(jnp.uint32)
    total = rows * count
    cols = width // count
    ranks = low_rank.shape[2]
    first_row, first_col = here * np.uint32(rows), here * np.uint32(cols)

    def my_cols(array):
        return cut(array, first_col, cols, array.ndim - 1)

    def my_rows(array):
        return cut(array, first_row, rows, 0)

    low = jnp.pad(low_rank, ((0, 0), (0, 0), (0, PAD - ranks))).transpose(1, 0, 2).reshape(-1, 2 * PAD)
    rank = lax.all_gather(low, ("seg", "seq"), axis=0, tiled=True)
    blocks = tm_mats[:4].reshape(4, -1, count, cols).transpose(2, 0, 1, 3)
    mine = exchange_seq(blocks.reshape(count, -1, cols), 0, 0).reshape(blocks.shape)
    mats = gather_seg(mine)
    x = gather_seq(tokens, 0, (mine, mats[segs // 2]))
    w_output = lax.all_gather(after(tm_mats[4], x), ("seg", "seq"), axis=0, tiled=True)
    go_cols = exchange_seq(after(out_grad, x), 1, 0)
    part = width // segs
    seg_starts = [(lax.axis_index("seg") ^ i) * part for i in range(segs)]
    at = jnp.stack([first_col.astype(jnp.int32)] + seg_starts)

    r, k, v, gp, rate, t, x_r, x_k, x_v, x_g = mix_forward(x, params, rank, at, mats)
    vec = my_cols(jnp.concatenate([params[9:12], jnp.zeros((5, width), F)], axis=0))
    groups = cols // LANES
    heads = cut(opening[0], here * np.uint32(cols // G), cols // G, 0)
    start = jnp.einsum(
        "ghkv,hi->ghvik", heads.reshape(groups, LANES // G, G, G), jnp.eye(LANES // G, dtype=F),
        precision=lax.Precision.HIGHEST,
    ).reshape(groups, LANES, LANES)
    r, go_cols = lax.optimization_barrier((r, go_cols))
    z_cols, y, states = wkv_forward(r, k, v, rate, gp, vec, start)
    z_held, z_far = ring_hops(z_cols)
    ring_cols = Ring(cols)
    z_at = jnp.stack([ring_cols.owner(away).astype(jnp.int32) for away in [a for a, _ in z_held] + [count // 2]])

    joined_mats = jnp.zeros((segs,) + mine.shape, HB)
    for i, value in enumerate(mats):
        joined_mats = put(joined_mats, value[None], {0: (lax.axis_index("seg") ^ i).astype(jnp.uint32)})
    joined_mats = joined_mats.reshape(segs * count, 4, -1, cols)
    down_t, up_t = rank[:, :PAD].T, rank[:, PAD:].T
    x_late, joined_mats, down_t, up_t = lax.optimization_barrier((x, joined_mats, down_t, up_t))
    x1, ck, cr, sg, gkv_cols = residual_forward(
        x_late, [piece for _, piece in z_held], z_far, z_at, w_output, params, cm_recept, go_cols
    )
    gkv = gather_seq(gkv_cols, 1)
    hp = mm(ck, cm_key)
    hid = jnp.square(jax.nn.relu(hp)).astype(HB)
    late = after(hid, gkv)
    kv = scatter_seq(lambda start: mm(late, cut(cm_value, start, cols, 1)), cols)
    cm_rows = exchange_seq((sg * kv).astype(HB), 0, 1)
    block_out = (my_rows(x1) + cm_rows.astype(F)).astype(HB)
    gsp = (go_cols.astype(F) * kv * sg * (1.0 - sg)).astype(HB)
    ghp = (mm_nt(gkv, cm_value) * (2.0 * jax.nn.relu(hp))).astype(HB)
    bit = seg_bit(1)
    near = [(i, i ^ 1) for i in range(segs)]

    def cm_half(a, b, which):
        size = a.shape[1] // 2
        return mm_tn(cut(a, which * np.uint32(size), size, 1), b).astype(HB)

    def cm_round(a, b):
        come = lax.ppermute(cm_half(a, b, np.uint32(1) - bit), "seg", near)
        return cm_half(a, b, bit), come

    cm_add = lambda pair: (pair[0].astype(F) + pair[1].astype(F)).astype(HB)
    values, keys = cm_add(cm_round(hid, gkv)), cm_add(cm_round(ck, ghp))
    recept = cm_round(cr, gsp)
    third, most = keys.shape[0] // 48 * 16, values.shape[0] // 48 * 32
    pump = Pump([(values[:most],)])
    token = pump.turn(gsp)
    gsp, ghp, _ = lax.optimization_barrier((gsp, ghp, (token, keys, recept[0])))
    go_own = put(jnp.zeros((total, width), HB), out_grad, {0: first_row})

    def piece_cols(array):
        return lambda start: cut(array, start, cols, 1).astype(F)

    start_row = jnp.zeros((8, width), F)
    gx1, gz_parts, sums_two, ahead = residual_backward(
        x1, go_own, ghp, gsp, cm_key, cm_recept, w_output, params, 0, 1, start_row, start_row
    )
    recept = cm_add(after(recept, ahead))
    pump.values += [(recept,), (keys[:third],), (keys[third : 2 * third],), (keys[2 * third :], values[most:])]
    ring = Scatter(piece_cols(gz_parts), cols)
    sent = ring.hop()
    token = pump.turn(sent)
    while ring.step > 0:
        sent = ring.hop(token)
        token = pump.turn(sent)
    gz = ring.finish(token)
    go1_cols = lax.psum_scatter(after(gx1, gz), "seq", scatter_dimension=1, tiled=True)

    adj = jnp.zeros((groups, LANES, LANES), F)
    sums = jnp.zeros((8, cols), F)
    outs = ()
    runs = 2
    run = total // runs
    for i in range(runs):
        outs, adj, sums = wkv_backward(r, k, v, rate, gp, y, gz, vec, states, total - (i + 1) * run, run, adj, sums, outs)
        sent = pump.turn(sums)
        adj = after(adj, (sent, block_out))
    gr, gk, gv, ggp, grb = outs
    d_four = jnp.stack([mm_tn(a, b).astype(HB) for a, b in ((x_r, gr), (x_k, gk), (x_v, gv), (x_g, ggp))])
    keep, come = seg_round(d_four.reshape(4, segs, -1, cols), 1, 1)
    tiles = total // 256
    splits = (tiles // 2, tiles // 4, tiles // 4)

    def mix(run, grad, given):
        return mix_backward(
            x, (grad, gk, gv, ggp, grb), t, gx1, joined_mats, rank, down_t, up_t, params, sums_two, sums,
            at, segs, tiles - 1 - sum(splits[:run]), splits[run], given,
        )

    while len(pump.done) < len(pump.values):
        sent = pump.turn(sums)
    (value_a,), (recept,), (key_a,), (key_b,), (key_c, value_b) = pump.done
    cm_sums = [jnp.concatenate([key_a, key_b, key_c], axis=0), jnp.concatenate([value_a, value_b], axis=0), recept]
    cm_come = [lax.ppermute(value, "seg", near) for value in cm_sums]
    d_four = (keep.astype(F) + come.astype(F)).astype(HB)
    keep, come = seg_round(d_four, 2, 1)
    gr, _ = lax.optimization_barrier((gr, (sent, keep)))
    out, ahead, packed = mix(0, gr, ())
    d_four = seg_rest(keep, after(come, ahead), 2, 1)
    d_four = exchange_seq(d_four.reshape(4, count, -1, cols).transpose(1, 0, 2, 3).reshape(count, -1, cols), 0, 0)
    go1_cols = after(go1_cols, ahead)
    d_out = outer_parts([piece for _, piece in z_held], z_far, z_at, go1_cols, width).reshape(segs, -1, cols)
    keep, come = seg_round(d_out, 1)
    d_out = (keep.astype(F) + come.astype(F)).astype(HB)
    keep, come = seg_round(d_out, 2)
    cm_come = after(cm_come, ahead)
    out, ahead, packed = mix(1, gr, (out, after(ahead, (keep, cm_come)), packed))
    d_out = exchange_seq(seg_rest(keep, after(come, ahead), 2).reshape(count, -1, cols), 0, 0)
    out, _, _, packed = mix(2, gr, (out, after(ahead, d_four), packed))
    d_out = after(d_out, packed)

    def joined(blocks, mats_in):
        return blocks.reshape(count, mats_in, -1, cols).transpose(1, 2, 0, 3).reshape(mats_in, -1, width).astype(F)

    d_mats = jnp.concatenate([joined(d_four, 4), joined(d_out, 1)], axis=0)
    rest = scatter_seg(packed).T
    final = Scatter(lambda start: cut(out, start, rows, 0).astype(F), rows)
    final.hop()
    which = bit.astype(jnp.int32).reshape(1)
    cm_grads = []
    for a, b in zip(cm_sums, cm_come):
        cm_grads.append(join_halves(after(a, packed), b, which))
        if final.step > 0:
            final.hop(cm_grads[-1])
    rest = exchange_seq(rest.reshape(count, -1, 2 * PAD), 0, 0).astype(F)
    input_grad = final.finish()
    rest = jnp.sum(rest, axis=0)
    rank_grad = jnp.stack([rest[:, :ranks], rest[:, PAD : PAD + ranks]])
    few = jnp.concatenate([rest[:, ranks:PAD], rest[:, PAD + ranks :]], axis=1).T
    vectors_grad = jnp.concatenate([few[0:3], few[32:37], few[17:18], few[16:17], few[18:20], few[8:12]], axis=0)
    return (block_out, input_grad, d_mats, rank_grad, vectors_grad, *cm_grads)


def solution(mesh):
    by_token = P(("seg", "seq"), None)
    in_specs = (
        by_token,
        P(None, ("seg", "seq"), None),
        P(None, ("seg", "seq"), None),
        P(),
        P("seg", None, None, None),
        P(None, "seq"),
        P("seq", None),
        P(None, "seq"),
        by_token,
    )
    out_specs = (
        by_token,
        by_token,
        P(None, ("seg", "seq"), None),
        P(None, ("seg", "seq"), None),
        P(None, ("seg", "seq")),
        P(None, "seq"),
        P("seq", None),
        P(None, "seq"),
    )
    return jax.shard_map(shards, mesh=mesh, in_specs=in_specs, out_specs=out_specs, check_vma=False)
```
